256 devices in a mesh: ctx: 32 (over z, y_hi, core), head: 8 (over x, y_lo).
Axes of the slice: x: 4, y: 4 (y_hi: 2, y_lo: 2; y = y_hi * 2 + y_lo), z: 8, core: 2. Of those that a mesh axis runs over, the one named last changes fastest.
Arguments:
- queries: bfloat16 [16384, 2048], P('ctx', 'head'), may hold values from -256 to 256
- rotated_key_rows: bfloat16 [16384, 1024], P('ctx', 'head'), may hold values from -8 to 8
- value_head_rows: bfloat16 [16384, 1024], P('ctx', 'head'), may hold values from -24 to 24
- stride_offset: int32 [16], P('head'), may hold values from 0 to 7
- w_out: bfloat16 [2048, 4096], P('head'), may hold values from -0.125 to 0.125
- grad_out: bfloat16 [16384, 4096], P('ctx', 'head'), may hold values from -6 to 6
Outputs:
- layer_out: bfloat16 [16384, 4096], P('ctx', 'head')
- grad_queries: bfloat16 [16384, 2048], P('ctx', 'head')
- key_gradient: bfloat16 [16384, 1024], P('ctx', 'head')
- value_gradient: bfloat16 [16384, 1024], P('ctx', 'head')
- grad_w_out: bfloat16 [2048, 4096], P('head', 'ctx')
The draws below stay inside these ranges and needn't reach their ends.
All inputs are finite; a program needn't handle non-finite values.
Results may differ from the reference program's by a relative error of at most 0.033.
Values may be sent and summed in bfloat16 or wider, within the bound.
A program may use at most 128 MiB of HBM per device.

```python
import math
import jax
import jax.numpy as jnp
from jax import lax

D = 4096
HEAD_SIZE = 128
QUERY_PER_KEY = 2
BLOCK_TOKENS = 64
LOCAL = 16
STRIDE = 8
TOKENS_PER_INDEX = 512
SEQUENCE_TOKENS = 16384
KEY_VALUE_HEADS = 8
HQ = 16
N_CTX = 32
N_HEAD = 8


def joint_draw(key):
    key_random_seed = jax.random.fold_in(key, 7)
    query_random_seed = jax.random.fold_in(key, 9)
    key_head_rows = jnp.clip(jax.random.normal(key_random_seed, (SEQUENCE_TOKENS, KEY_VALUE_HEADS, HEAD_SIZE), jnp.float32), -4.0, 4.0)
    query_head_rows = jnp.clip(1.5 * jax.random.normal(query_random_seed, (SEQUENCE_TOKENS, KEY_VALUE_HEADS, QUERY_PER_KEY, HEAD_SIZE), jnp.float32), -9.0, 9.0)
    return (query_head_rows.reshape(SEQUENCE_TOKENS, KEY_VALUE_HEADS * QUERY_PER_KEY * HEAD_SIZE), key_head_rows.reshape(SEQUENCE_TOKENS, KEY_VALUE_HEADS * HEAD_SIZE))


def draw_queries(key, part):
    return joint_draw(key)[0].astype(jnp.bfloat16)


def draw_rotated_key_rows(key, part):
    return joint_draw(key)[1].astype(jnp.bfloat16)


def with_ends(drawn, own_key, smallest, top_value):
    shape = drawn.shape
    spot = [jax.random.randint(jax.random.fold_in(own_key, axis), (), 0, shape[axis]) for axis in range(len(shape))]
    drawn = drawn.at[tuple(spot)].set(smallest)
    longest = shape.index(max(shape))
    spot[longest] = (spot[longest] + 1) % shape[longest]
    return drawn.at[tuple(spot)].set(top_value)


def with_spikes(drawn, rng, source, target, shards_of, factor):
    def block_of(dim):
        return (jnp.arange(drawn.shape[dim]) // (drawn.shape[dim] // shards_of)).reshape((-1,) + (1,) * (drawn.ndim - 1 - dim))

    one_side = jax.random.permutation(rng, shards_of)[block_of(target)]
    other_side = (block_of(target) + shards_of // 2) % shards_of
    return jnp.where((block_of(source) == one_side) | (block_of(source) == other_side), factor * drawn, drawn)


def block_scale(own_key, dims, cuts, least, high):
    level, own = 1.0, jax.random.fold_in(own_key, 6)
    for axis_at, blocks in cuts:
        draws = jnp.exp(jax.random.uniform(jax.random.fold_in(own, axis_at), (blocks,), jnp.float32, least / len(cuts), high / len(cuts)))
        level = level * jnp.repeat(draws, dims[axis_at] // blocks).reshape([-1 if axis == axis_at else 1 for axis in range(len(dims))])
    return level


def noise(own_key, shape, width, limit, cuts=(), held_as=jnp.bfloat16):
    entries = width * jax.random.normal(own_key, shape, jnp.float32)
    if cuts:
        entries = entries * block_scale(own_key, shape, cuts, -0.22, 0.18)
    return jnp.clip(entries, -limit, limit).astype(held_as)


def noise_with(key, dims, width, most, pieces, heavy, held_as=jnp.bfloat16):
    values = width * jax.random.normal(key, dims, jnp.float32)
    if pieces:
        values = values * block_scale(key, dims, pieces, -0.22, 0.18)
    return jnp.clip(with_spikes(values, jax.random.fold_in(key, 3), *heavy), -most, most).astype(held_as)


def setup_inputs(seed: int = 0) -> dict:
    key_list = jax.random.split(jax.random.key(seed), 7)
    queries = draw_queries(jax.random.fold_in(key_list[6], 71), 0)
    rotated_key_rows = draw_rotated_key_rows(jax.random.fold_in(key_list[6], 71), 0)
    value_head_rows = noise(key_list[2], (SEQUENCE_TOKENS, KEY_VALUE_HEADS * HEAD_SIZE), 4.0, 24.0, ((0, 32), (1, 8)))
    stride_offset = with_ends(jax.random.randint(key_list[3], (HQ,), 0, STRIDE), jax.random.fold_in(key_list[3], 1), 0, STRIDE - 1).astype(jnp.int32)
    w_out = noise(key_list[4], (HQ * HEAD_SIZE, D), (HQ * HEAD_SIZE) ** -0.5, 0.125, ((0, 8),))
    grad_out = noise_with(key_list[5], (SEQUENCE_TOKENS, D), 1.0, 6.0, ((0, 32), (1, 8)), (0, 1, 32, 2.75))
    return dict(queries=queries, rotated_key_rows=rotated_key_rows, value_head_rows=value_head_rows, stride_offset=stride_offset, w_out=w_out, grad_out=grad_out)


def contract_rows(form, left, right):
    return jnp.einsum(form, left, right, precision=lax.Precision.HIGHEST)


def to_low(values):
    return lax.optimization_barrier(values.astype(jnp.bfloat16)).astype(jnp.float32)


def band_allowed(shard_id, phase_list):
    tokens_q = shard_id * TOKENS_PER_INDEX + jnp.arange(TOKENS_PER_INDEX, dtype=jnp.int32)
    tokens_k = (shard_id - 2) * TOKENS_PER_INDEX + jnp.arange(3 * TOKENS_PER_INDEX, dtype=jnp.int32)
    block_q = tokens_q // BLOCK_TOKENS
    block_k = tokens_k // BLOCK_TOKENS
    causal = (tokens_k[None, :] >= 0) & (tokens_k[None, :] <= tokens_q[:, None])
    nearby = (block_q[:, None] - block_k[None, :]) < LOCAL
    on_stride = ((block_k[None, None, :] + phase_list[:, :, None]) % STRIDE) == STRIDE - 1
    return causal[None, None] & (nearby[None, None] | on_stride[:, :, None, :])


def pick_rows(source, select_mask):
    grouped = source.reshape(-1, STRIDE, BLOCK_TOKENS, source.shape[1], HEAD_SIZE)
    chosen = contract_rows('grs,nsbgd->grnbd', select_mask, grouped)
    return chosen.reshape(chosen.shape[0], chosen.shape[1], -1, HEAD_SIZE)


def reference(queries, rotated_key_rows, value_head_rows, stride_offset, w_out, grad_out):
    scaling = HEAD_SIZE ** -0.5
    phase_list = stride_offset.reshape(KEY_VALUE_HEADS, QUERY_PER_KEY)
    select_mask = (jnp.arange(STRIDE, dtype=jnp.int32)[None, None, :] == (STRIDE - 1 - phase_list)[:, :, None]).astype(jnp.float32)
    query_all_rows = queries.astype(jnp.float32).reshape(SEQUENCE_TOKENS, KEY_VALUE_HEADS, QUERY_PER_KEY, HEAD_SIZE)
    key_all_rows = rotated_key_rows.astype(jnp.float32).reshape(SEQUENCE_TOKENS, KEY_VALUE_HEADS, HEAD_SIZE)
    value_all_rows = value_head_rows.astype(jnp.float32).reshape(SEQUENCE_TOKENS, KEY_VALUE_HEADS, HEAD_SIZE)
    filler_value = jnp.zeros((2 * TOKENS_PER_INDEX, KEY_VALUE_HEADS, HEAD_SIZE), jnp.float32)
    padded_k = jnp.concatenate([filler_value, key_all_rows], axis=0)
    padded_v = jnp.concatenate([filler_value, value_all_rows], axis=0)
    picked_k = pick_rows(key_all_rows, select_mask)
    picked_v = pick_rows(value_all_rows, select_mask)
    picked_rows = TOKENS_PER_INDEX // STRIDE
    picked_count = picked_rows * N_CTX
    tile_rows = BLOCK_TOKENS * math.gcd(picked_count // BLOCK_TOKENS, max(1, 512 // BLOCK_TOKENS))
    tile_count = picked_count // tile_rows

    def shard_inputs(shard_id):
        q_t = lax.dynamic_slice_in_dim(query_all_rows, shard_id * TOKENS_PER_INDEX, TOKENS_PER_INDEX, 0)
        near_k = lax.dynamic_slice_in_dim(padded_k, shard_id * TOKENS_PER_INDEX, 3 * TOKENS_PER_INDEX, 0)
        near_v = lax.dynamic_slice_in_dim(padded_v, shard_id * TOKENS_PER_INDEX, 3 * TOKENS_PER_INDEX, 0)
        return q_t, near_k, near_v, band_allowed(shard_id, phase_list), (shard_id - 2) * picked_rows

    def keep_state(running):
        return running

    def forward_shard(shard_id):
        q_t, near_k, near_v, allowed, bound_rows = shard_inputs(shard_id)
        scores = jnp.where(allowed, contract_rows('tgrd,ugd->grtu', q_t, near_k) * scaling, -jnp.inf)
        row_max = jnp.max(scores, axis=-1)
        weights = jnp.where(allowed, jnp.exp(scores - row_max[..., None]), 0.0)
        row_sum = jnp.sum(weights, axis=-1)
        weighted = contract_rows('grtu,ugd->grtd', to_low(weights), near_v)

        def tile_step(tile_index, running):
            tile_start = tile_index * tile_rows

            def update(running):
                row_max, row_sum, weighted = running
                tile_k = lax.dynamic_slice_in_dim(picked_k, tile_start, tile_rows, 2)
                tile_v = lax.dynamic_slice_in_dim(picked_v, tile_start, tile_rows, 2)
                usable = (tile_start + jnp.arange(tile_rows, dtype=jnp.int32)) < bound_rows
                scores = jnp.where(usable, contract_rows('tgrd,grkd->grtk', q_t, tile_k) * scaling, -jnp.inf)
                new_max = jnp.maximum(row_max, jnp.max(scores, axis=-1))
                weights = jnp.where(usable, jnp.exp(scores - new_max[..., None]), 0.0)
                factor = jnp.exp(row_max - new_max)
                row_sum = row_sum * factor + jnp.sum(weights, axis=-1)
                weighted = weighted * factor[..., None] + contract_rows('grtk,grkd->grtd', to_low(weights), tile_v)
                return new_max, row_sum, weighted

            return lax.cond(tile_start < bound_rows, update, keep_state, running)

        row_max, row_sum, weighted = lax.fori_loop(0, tile_count, tile_step, (row_max, row_sum, weighted))
        mixed = weighted / row_sum[..., None]
        return jnp.transpose(mixed, (2, 0, 1, 3)).astype(jnp.bfloat16), row_max + jnp.log(row_sum)

    shard_outs, shard_logs = lax.map(forward_shard, jnp.arange(N_CTX, dtype=jnp.int32))
    attended_rows = shard_outs.reshape(SEQUENCE_TOKENS, HQ * HEAD_SIZE)
    width_group = HQ * HEAD_SIZE // N_HEAD
    heads_sum = jnp.zeros((SEQUENCE_TOKENS, D), jnp.float32)
    for group_id in range(N_HEAD):
        head_term = jnp.dot(attended_rows[:, group_id * width_group:(group_id + 1) * width_group], w_out[group_id * width_group:(group_id + 1) * width_group], preferred_element_type=jnp.float32)
        heads_sum = heads_sum + to_low(head_term)
    layer_out = heads_sum.astype(jnp.bfloat16)
    grad_w_out = jnp.dot(attended_rows.T, grad_out, preferred_element_type=jnp.float32).astype(jnp.bfloat16)
    attention_gradient = jnp.dot(grad_out, w_out.T, preferred_element_type=jnp.float32).astype(jnp.bfloat16)
    output_gradient_all = attention_gradient.astype(jnp.float32).reshape(SEQUENCE_TOKENS, KEY_VALUE_HEADS, QUERY_PER_KEY, HEAD_SIZE)
    output_all_rows = attended_rows.astype(jnp.float32).reshape(SEQUENCE_TOKENS, KEY_VALUE_HEADS, QUERY_PER_KEY, HEAD_SIZE)

    def backward_shard(running, shard_id):
        key_accumulator, value_accumulator = running
        q_t, near_k, near_v, allowed, bound_rows = shard_inputs(shard_id)
        do_t = lax.dynamic_slice_in_dim(output_gradient_all, shard_id * TOKENS_PER_INDEX, TOKENS_PER_INDEX, 0)
        o_t = lax.dynamic_slice_in_dim(output_all_rows, shard_id * TOKENS_PER_INDEX, TOKENS_PER_INDEX, 0)
        log_t = shard_logs[shard_id]
        row_dot = jnp.transpose(jnp.sum(do_t * o_t, axis=-1), (1, 2, 0))
        scores = contract_rows('tgrd,ugd->grtu', q_t, near_k) * scaling
        weights = jnp.where(allowed, jnp.exp(scores - log_t[..., None]), 0.0)
        grad_near_v = contract_rows('grtu,tgrd->ugd', to_low(weights), do_t)
        grad_weights = contract_rows('tgrd,ugd->grtu', do_t, near_v)
        grad_scores = to_low(weights * (grad_weights - row_dot[..., None]))
        grad_q = contract_rows('grtu,ugd->tgrd', grad_scores, near_k) * scaling
        grad_near_k = contract_rows('grtu,tgrd->ugd', grad_scores, q_t) * scaling

        def tile_step(tile_index, inner):
            tile_start = tile_index * tile_rows

            def update(inner):
                grad_q, grad_pk, grad_pv = inner
                tile_k = lax.dynamic_slice_in_dim(picked_k, tile_start, tile_rows, 2)
                tile_v = lax.dynamic_slice_in_dim(picked_v, tile_start, tile_rows, 2)
                usable = (tile_start + jnp.arange(tile_rows, dtype=jnp.int32)) < bound_rows
                scores = contract_rows('tgrd,grkd->grtk', q_t, tile_k) * scaling
                weights = jnp.where(usable, jnp.exp(scores - log_t[..., None]), 0.0)
                tile_gv = contract_rows('grtk,tgrd->grkd', to_low(weights), do_t)
                grad_weights = contract_rows('tgrd,grkd->grtk', do_t, tile_v)
                grad_scores = to_low(weights * (grad_weights - row_dot[..., None]))
                grad_q = grad_q + contract_rows('grtk,grkd->tgrd', grad_scores, tile_k) * scaling
                tile_gk = contract_rows('grtk,tgrd->grkd', grad_scores, q_t) * scaling
                grad_pk = lax.dynamic_update_slice_in_dim(grad_pk, tile_gk, tile_start, 2)
                grad_pv = lax.dynamic_update_slice_in_dim(grad_pv, tile_gv, tile_start, 2)
                return grad_q, grad_pk, grad_pv

            return lax.cond(tile_start < bound_rows, update, keep_state, inner)

        empty_state = jnp.zeros((KEY_VALUE_HEADS, QUERY_PER_KEY, picked_count, HEAD_SIZE), jnp.float32)
        grad_q, grad_pk, grad_pv = lax.fori_loop(0, tile_count, tile_step, (grad_q, empty_state, empty_state))

        def place(picked_gradient, grad_near):
            spread_row_list = contract_rows('xij,xiucz->ujcxz', select_mask, picked_gradient.reshape(KEY_VALUE_HEADS, QUERY_PER_KEY, -1, BLOCK_TOKENS, HEAD_SIZE)).reshape(SEQUENCE_TOKENS, KEY_VALUE_HEADS, HEAD_SIZE)
            padded = jnp.concatenate([filler_value, spread_row_list], axis=0)
            region = lax.dynamic_slice_in_dim(padded, shard_id * TOKENS_PER_INDEX, 3 * TOKENS_PER_INDEX, 0) + grad_near
            padded = lax.dynamic_update_slice_in_dim(padded, region, shard_id * TOKENS_PER_INDEX, 0)
            return to_low(padded[2 * TOKENS_PER_INDEX:])

        key_accumulator = key_accumulator + place(grad_pk, grad_near_k)
        value_accumulator = value_accumulator + place(grad_pv, grad_near_v)
        return (key_accumulator, value_accumulator), grad_q.astype(jnp.bfloat16)

    initial_accumulator = jnp.zeros((SEQUENCE_TOKENS, KEY_VALUE_HEADS, HEAD_SIZE), jnp.float32)
    (key_accumulator, value_accumulator), grad_shards = lax.scan(backward_shard, (initial_accumulator, initial_accumulator), jnp.arange(N_CTX, dtype=jnp.int32))
    grad_queries = grad_shards.reshape(SEQUENCE_TOKENS, HQ * HEAD_SIZE)
    key_gradient = key_accumulator.astype(jnp.bfloat16).reshape(SEQUENCE_TOKENS, KEY_VALUE_HEADS * HEAD_SIZE)
    value_gradient = value_accumulator.astype(jnp.bfloat16).reshape(SEQUENCE_TOKENS, KEY_VALUE_HEADS * HEAD_SIZE)
    return (layer_out, grad_queries, key_gradient, value_gradient, grad_w_out)
```

```python
import jax
import jax.numpy as jnp
from jax import lax
from jax.experimental import pallas as pl
from jax.experimental.pallas import tpu as pltpu
from jax.sharding import PartitionSpec as P

T = 512
DH = 128
BLK = 64
NH = 8
NC = 32
SCALE = DH ** -0.5
EXP2_SCALE = SCALE * 1.4426950408889634
NEG = -1e30
MESH = pl.DeviceIdType.MESH
BF = jnp.bfloat16
F32 = jnp.float32


def where_am_i():
    c = lax.axis_index("ctx")
    h = lax.axis_index("head")
    return c, h, c // 4, (c // 2) % 2, c % 2


def ctx_id(z, yh, core):
    return z * 4 + yh * 2 + core


def signal(barrier, c, h):
    pl.semaphore_signal(barrier, inc=1, device_id=(c, h), device_id_type=MESH)


class Sends:
    def __init__(self, sems):
        self.sems, self.made = sems, []

    def start(self, src, dst, recv, c, h):
        copy = pltpu.make_async_remote_copy(
            src_ref=src, dst_ref=dst, send_sem=self.sems.at[len(self.made)],
            recv_sem=recv, device_id=(c, h), device_id_type=MESH)
        copy.start()
        self.made.append(copy)

    def finish(self):
        for copy in self.made:
            copy.wait_send()


def arrived(ref, recv, send, c, h):
    pltpu.make_async_remote_copy(
        src_ref=ref, dst_ref=ref, send_sem=send, recv_sem=recv,
        device_id=(c, h), device_id_type=MESH).wait_recv()


def gather_kernel(off_ref, k_ref, v_ref, w_ref, picked, near, wc,
                  send, pk_recv, w_recv, c_recv, b_recv, local):
    c, h, z, yh, core = where_am_i()
    partner = c + 1 - 2 * core
    ypeer = ctx_id(z, 1 - yh, core)
    after, before = lax.rem(c + 2, NC), lax.rem(c + NC - 2, NC)
    barrier = pltpu.get_barrier_semaphore()
    zs = [ctx_id(lax.rem(z + d, 8), yh, core) for d in (1, 7, 2, 6, 3, 5, 4)]
    zys = [ctx_id(lax.rem(z + d, 8), 1 - yh, core) for d in (1, 7, 2, 6, 3, 5, 4)]
    hs = [lax.rem(h + d, NH) for d in range(1, NH)]
    for peer in [partner, ypeer, after, before] + zs:
        signal(barrier, peer, h)
    for peer in hs:
        signal(barrier, c, peer)
    for r in range(2):
        wanted = jnp.full((BLK, DH), 7 - off_ref[r], jnp.int32)
        for source, slot in ((k_ref, r), (v_ref, 2 + r)):
            rows = source[:BLK].astype(F32)
            for b in range(1, 8):
                rows = jnp.where(wanted == b, source[b * BLK:(b + 1) * BLK].astype(F32), rows)
            picked[slot, c] = rows.astype(BF)
    copies = [
        pltpu.make_async_copy(k_ref, near.at[0, 0], local.at[0]),
        pltpu.make_async_copy(v_ref, near.at[1, 0], local.at[1]),
        pltpu.make_async_copy(
            w_ref.at[:, pl.ds(pl.multiple_of(h * T, T), T)],
            wc.at[pl.ds(pl.multiple_of(h * 256, 256), 256), :], local.at[2]),
    ]
    for copy in copies:
        copy.start()
    pl.semaphore_wait(barrier, 4 + 7 + 7)

    sends = Sends(send)

    def block(t):
        return picked.at[:, t]

    def piece(half, r):
        return wc.at[pl.ds(pl.multiple_of(r * 256, 256), 256),
                     pl.ds(pl.multiple_of(half * 256, 256), 256)]

    sends.start(block(c), block(c), pk_recv.at[c], ypeer, h)
    sends.start(k_ref, near.at[0, 2], c_recv.at[0], after, h)
    sends.start(v_ref, near.at[1, 2], c_recv.at[1], after, h)
    for n in range(7):
        sends.start(block(c), block(c), pk_recv.at[c], zs[n], h)
        sends.start(
            w_ref.at[:, pl.ds(pl.multiple_of(hs[n] * T + core * 256, 256), 256)],
            piece(core, h), w_recv.at[core, h], c, hs[n])
    sends.start(block(c), block(c), pk_recv.at[c], partner, h)

    arrived(block(ypeer), pk_recv.at[ypeer], send.at[0], ypeer, h)
    for n in range(7):
        sends.start(block(ypeer), block(ypeer), pk_recv.at[ypeer], zs[n], h)
    sends.start(block(ypeer), block(ypeer), pk_recv.at[ypeer], partner, h)

    arrived(near.at[0, 2], c_recv.at[0], send.at[0], before, h)
    arrived(near.at[1, 2], c_recv.at[1], send.at[0], before, h)
    for copy in copies:
        copy.wait()
    give = 2 * core
    sends.start(near.at[0, give], near.at[0, 1], b_recv.at[0], partner, h)
    sends.start(near.at[1, give], near.at[1, 1], b_recv.at[1], partner, h)
    for n in range(7):
        arrived(piece(core, hs[n]), w_recv.at[core, hs[n]], send.at[0], c, hs[n])
        sends.start(piece(core, hs[n]), piece(core, hs[n]), w_recv.at[core, hs[n]], partner, h)
        arrived(block(zs[n]), pk_recv.at[zs[n]], send.at[0], zs[n], h)
        sends.start(block(zs[n]), block(zs[n]), pk_recv.at[zs[n]], partner, h)
    for n in range(7):
        arrived(block(zys[n]), pk_recv.at[zys[n]], send.at[0], zs[n], h)
        sends.start(block(zys[n]), block(zys[n]), pk_recv.at[zys[n]], partner, h)
    flip = 1 - 2 * core
    for t in [c, ypeer] + zs + zys:
        arrived(block(t + flip), pk_recv.at[t + flip], send.at[0], partner, h)
    for n in range(7):
        arrived(piece(1 - core, hs[n]), w_recv.at[1 - core, hs[n]], send.at[0], partner, h)
    arrived(near.at[0, 1], b_recv.at[0], send.at[0], partner, h)
    arrived(near.at[1, 1], b_recv.at[1], send.at[0], partner, h)
    sends.finish()


def fold(x, op):
    return op(x.reshape(T // 8, 8, T), axis=0)


def nt(a, b):
    return lax.dot_general(a, b, (((1,), (1,)), ((), ())), preferred_element_type=F32)


def tn(a, b):
    return lax.dot_general(a, b, (((0,), (0,)), ((), ())), preferred_element_type=F32)


def nn(a, b):
    return jnp.dot(a, b, preferred_element_type=F32)


def attention_kernel(off_ref, q_ref, near, picked, gpart,
                     att_all, gq_ref, gnear, gpick,
                     qs, scores, probs, grecv, dnear, top, inv, acc, dog,
                     send, g_recv, a_recv):
    c, h, z, yh, core = where_am_i()
    barrier = pltpu.get_barrier_semaphore()
    hs = [lax.rem(h + d, NH) for d in range(1, NH)]
    for peer in hs:
        signal(barrier, c, peer)
    for r in range(2):
        qs[r] = q_ref[:, r * DH:(r + 1) * DH]
    dnear[...] = jnp.zeros_like(dnear)
    pl.semaphore_wait(barrier, 7)
    sends = Sends(send)
    for peer in hs:
        sends.start(gpart.at[peer], grecv.at[h], g_recv.at[h], c, peer)

    def tile(p):
        return pl.ds(pl.multiple_of(p * 8, 8), 8)

    def forward(r, _):
        q = qs[r]
        key = lax.broadcasted_iota(jnp.int32, (T, T), 0)
        query = lax.broadcasted_iota(jnp.int32, (T, T), 1)
        s = jnp.where(key <= query, nt(near[0, 0], q), NEG)
        scores[0] = s
        top[...] = fold(s, jnp.max)
        s = jnp.where(c >= 1, nt(near[0, 1], q), NEG)
        scores[1] = s
        top[...] = jnp.maximum(top[...], fold(s, jnp.max))
        kb, qb = key // BLK, query // BLK
        ok = ((kb > qb) | (kb == 7 - off_ref[r])) & (c >= 2)
        s = jnp.where(ok, nt(near[0, 2], q), NEG)
        scores[2] = s
        top[...] = jnp.maximum(top[...], fold(s, jnp.max))

        def pick_scores(p, _):
            rows = lax.broadcasted_iota(jnp.int32, (T, T), 0)
            s = nt(picked[r, tile(p)].reshape(T, DH), q)
            s = jnp.where(rows < (c - 2) * BLK - p * T, s, NEG)
            scores[3 + p] = s
            top[...] = jnp.maximum(top[...], fold(s, jnp.max))
            return 0

        lax.fori_loop(0, 4, pick_scores, 0)
        m = jnp.max(top[...], axis=0, keepdims=True)
        top[...] = jnp.zeros_like(top)
        acc[...] = jnp.zeros_like(acc)

        def weigh(i, values):
            w = jnp.exp2((scores[i] - m) * EXP2_SCALE)
            top[...] += fold(w, jnp.sum)
            w = w.astype(BF)
            probs[r, i] = w
            acc[...] += tn(values, w)

        def near_mix(i, _):
            weigh(i, near[1, i])
            return 0

        def pick_mix(p, _):
            weigh(3 + p, picked[2 + r, tile(p)].reshape(T, DH))
            return 0

        lax.fori_loop(0, 3, near_mix, 0)
        lax.fori_loop(0, 4, pick_mix, 0)
        total = 1.0 / jnp.sum(top[...], axis=0, keepdims=True)
        inv[r] = jnp.broadcast_to(total, (8, T))
        att_all[h, pl.ds(pl.multiple_of(r * DH, DH), DH), :] = (acc[...] * total).astype(BF)
        return 0

    lax.fori_loop(0, 2, forward, 0)
    for peer in hs:
        sends.start(att_all.at[h], att_all.at[h], a_recv.at[h], c, peer)
    for peer in hs:
        arrived(grecv.at[peer], g_recv.at[peer], send.at[0], c, peer)

    def backward(r, _):
        rows = pl.ds(pl.multiple_of(r * DH, DH), DH)
        grad = gpart[h, rows, :].astype(F32)
        for peer in hs:
            grad += grecv[peer, rows, :].astype(F32)
        grad = grad.astype(BF).astype(F32)
        total = inv[r, 0:1]
        rowdot = jnp.sum(grad * att_all[h, rows, :].astype(F32), axis=0, keepdims=True) * total
        dog[...] = (grad * total).T.astype(BF)
        acc[...] = jnp.zeros_like(acc)

        def grads(i, keys, values):
            w = probs[r, i]
            do = dog[...]
            dp = nt(values, do)
            ds = (w.astype(F32) * (dp - rowdot)).astype(BF)
            acc[...] += tn(keys, ds)
            return nn(ds, qs[r]) * SCALE, nn(w, do)

        def near_grads(i, _):
            dk, dv = grads(i, near[0, i], near[1, i])
            dnear[0, i] += dk
            dnear[1, i] += dv
            return 0

        def pick_grads(p, _):
            dk, dv = grads(3 + p, picked[r, tile(p)].reshape(T, DH),
                           picked[2 + r, tile(p)].reshape(T, DH))
            gpick[r, tile(p)] = dk.astype(BF).reshape(8, BLK, DH)
            gpick[2 + r, tile(p)] = dv.astype(BF).reshape(8, BLK, DH)
            return 0

        lax.fori_loop(0, 3, near_grads, 0)
        lax.fori_loop(0, 4, pick_grads, 0)
        qs[r] = (acc[...].T * SCALE).astype(BF)
        return 0

    lax.fori_loop(0, 2, backward, 0)
    for r in range(2):
        gq_ref[:, r * DH:(r + 1) * DH] = qs[r]
    gnear[...] = dnear[...].astype(BF)
    for peer in hs:
        arrived(att_all.at[peer], a_recv.at[peer], send.at[0], c, peer)
    sends.finish()


def scatter_kernel(off_ref, wt, gpick, gnear, gk_ref, gv_ref, gw_ref,
                   wrecv, wsum, wslot, precv, psum, pslot, brecv, csum, crecv,
                   send, pair_recv, w_recv, p_recv, c_recv, local):
    c, h, z, yh, core = where_am_i()
    partner = c + 1 - 2 * core
    after, before = lax.rem(c + 2, NC), lax.rem(c + NC - 2, NC)
    barrier = pltpu.get_barrier_semaphore()
    places = [(d, y) for d in (4, 3, 5, 2, 6, 1, 7, 0) for y in (1, 0)]
    ids = []
    for d, y in places:
        zz = lax.rem(z + d, 8)
        yy = lax.rem(yh + y, 2)
        ids.append((zz, yy, ctx_id(zz, yy, core)))
    me = z * 2 + yh

    def dest(n):
        r = lax.rem(h + places[n][0], NH)
        y = lax.rem(yh + places[n][1], 2)
        return r, y, ctx_id(h, y, core)

    signal(barrier, partner, h)
    signal(barrier, after, h)
    signal(barrier, before, h)
    for n in range(15):
        signal(barrier, ids[n][2], h)
    for n in range(16):
        r, y, t = dest(n)

        @pl.when((t != c) | (r != h))
        def _():
            signal(barrier, t, r)

        source = ids[n][2]

        @pl.when((source != c) | (z != h))
        def _():
            signal(barrier, source, z)

    pl.semaphore_wait(barrier, jnp.where(z == h, 18 + 30, 18 + 32))

    sends = Sends(send)
    sends.start(gnear.at[:, 1], brecv, pair_recv.at[0], partner, h)
    sends.start(gpick.at[:, :, 1 - core], precv, pair_recv.at[1], partner, h)
    for y in range(2):
        sends.start(wt.at[:, pl.ds(pl.multiple_of((2 * y + 1 - core) * DH, DH), DH)],
                    wrecv.at[y], pair_recv.at[2 + y], partner, h)

    arrived(brecv, pair_recv.at[0], send.at[0], partner, h)
    extra = brecv[...].astype(F32)
    isodd = (core == 1)
    csum[...] = (gnear[:, 2].astype(F32) + jnp.where(isodd, extra, 0.0)).astype(BF)
    arrived(precv, pair_recv.at[1], send.at[0], partner, h)

    def pick_sum(n, _):
        psum[:, n] = (gpick[:, n, core].astype(F32) + precv[:, n].astype(F32)).astype(BF)
        return 0

    lax.fori_loop(0, 16, pick_sum, 0)
    sends.start(csum, crecv, c_recv.at[0], before, h)
    for n in range(15):
        zz, yy, t = ids[n]
        sends.start(psum.at[:, zz * 2 + yy], pslot.at[me], p_recv.at[me], t, h)

    for y in range(2):
        arrived(wrecv.at[y], pair_recv.at[2 + y], send.at[0], partner, h)
        mine = wt[:, pl.ds(pl.multiple_of((2 * y + core) * DH, DH), DH)]
        wsum[y] = (mine.astype(F32) + wrecv[y].astype(F32)).astype(BF)
    base = len(sends.made)

    def w_copy(n):
        r, y, t = dest(n)
        rows = pl.ds(pl.multiple_of(r * 256, 256), 256)
        return (r, t), wsum.at[y, rows, :], pltpu.make_async_remote_copy(
            src_ref=wsum.at[y, rows, :], dst_ref=wslot.at[me],
            send_sem=send.at[base + n], recv_sem=w_recv.at[me],
            device_id=(t, r), device_id_type=MESH)

    for n in range(16):
        (r, t), src, copy = w_copy(n)

        @pl.when((t != c) | (r != h))
        def _():
            copy.start()

        @pl.when((t == c) & (r == h))
        def _():
            own = pltpu.make_async_copy(src, wslot.at[me], local)
            own.start()
            own.wait()

    arrived(crecv, c_recv.at[0], send.at[0], after, h)
    grad = gnear[:, 0].astype(F32) + jnp.where(isodd, 0.0, extra) + crecv[...].astype(F32)
    for n in range(15):
        zz, yy, t = ids[n]
        arrived(pslot.at[zz * 2 + yy], p_recv.at[zz * 2 + yy], send.at[0], t, h)
    pslot[me] = psum[:, me]
    total = pslot[0].astype(F32)
    for n in range(1, 16):
        total += pslot[n].astype(F32)
    block = lax.broadcasted_iota(jnp.int32, (T, DH), 0) // BLK
    for n, out in enumerate((gk_ref, gv_ref)):
        g = grad[n]
        for r in range(2):
            spread = jnp.concatenate([total[2 * n + r]] * 8, axis=0)
            g += jnp.where(block == 7 - off_ref[r], spread, 0.0)
        out[...] = g.astype(BF)
    for n in range(16):
        zz, yy, source = ids[n]

        @pl.when((source != c) | (z != h))
        def _():
            arrived(wslot.at[zz * 2 + yy], w_recv.at[zz * 2 + yy], send.at[0], source, z)

    total = wslot[0].astype(F32)
    for n in range(1, 16):
        total += wslot[n].astype(F32)
    gw_ref[...] = total.astype(BF)
    sends.finish()
    for n in range(16):
        (r, t), src, copy = w_copy(n)

        @pl.when((t != c) | (r != h))
        def _():
            copy.wait_send()


VM = pl.BlockSpec(memory_space=pltpu.VMEM)
SM = pl.BlockSpec(memory_space=pltpu.SMEM)
DMA = pltpu.SemaphoreType.DMA


def shaped(*shape, dtype=BF):
    return jax.ShapeDtypeStruct(shape, dtype)


def params(number):
    return pltpu.CompilerParams(
        collective_id=number, has_side_effects=True, vmem_limit_bytes=60 << 20)


def body(queries, keys, values, stride_offset, w_out, grad_out):
    picked, near, wc = pl.pallas_call(
        gather_kernel,
        out_shape=(shaped(4, NC, BLK, DH), shaped(2, 3, T, DH), shaped(2048, T)),
        in_specs=[SM, VM, VM, VM],
        out_specs=(VM, VM, VM),
        scratch_shapes=[DMA((54,)), DMA((NC,)), DMA((2, NH)), DMA((2,)), DMA((2,)), DMA((3,))],
        compiler_params=params(0),
        name="gather_rows",
    )(stride_offset, keys, values, w_out)
    gpart = lax.dot_general(wc, grad_out, (((1,), (1,)), ((), ())), preferred_element_type=F32)
    gpart = gpart.astype(BF).reshape(NH, 256, T)
    att_all, grad_queries, gnear, gpick = pl.pallas_call(
        attention_kernel,
        out_shape=(shaped(NH, 256, T), shaped(T, 256), shaped(2, 3, T, DH),
                   shaped(4, NC, BLK, DH)),
        in_specs=[SM, VM, VM, VM, VM],
        out_specs=(VM, VM, VM, VM),
        scratch_shapes=[
            pltpu.VMEM((2, T, DH), BF), pltpu.VMEM((7, T, T), F32),
            pltpu.VMEM((2, 7, T, T), BF), pltpu.VMEM((NH, 256, T), BF),
            pltpu.VMEM((2, 3, T, DH), F32), pltpu.VMEM((8, T), F32),
            pltpu.VMEM((2, 8, T), F32), pltpu.VMEM((DH, T), F32), pltpu.VMEM((T, DH), BF),
            DMA((14,)), DMA((NH,)), DMA((NH,)),
        ],
        compiler_params=params(1),
        name="attend",
    )(stride_offset, queries, near, picked, gpart)
    att = att_all.reshape(2048, T)
    layer_out = lax.dot_general(
        att, wc, (((0,), (0,)), ((), ())), preferred_element_type=F32).astype(BF)
    wt = jnp.dot(att, grad_out, preferred_element_type=F32).astype(BF)
    gk, gv, gw = pl.pallas_call(
        scatter_kernel,
        out_shape=(shaped(T, DH), shaped(T, DH), shaped(256, DH)),
        in_specs=[SM, VM, VM, VM],
        out_specs=(VM, VM, VM),
        scratch_shapes=[
            pltpu.VMEM((2, 2048, DH), BF), pltpu.VMEM((2, 2048, DH), BF),
            pltpu.VMEM((16, 256, DH), BF), pltpu.VMEM((4, 16, BLK, DH), BF),
            pltpu.VMEM((4, 16, BLK, DH), BF), pltpu.VMEM((16, 4, BLK, DH), BF),
            pltpu.VMEM((2, T, DH), BF), pltpu.VMEM((2, T, DH), BF), pltpu.VMEM((2, T, DH), BF),
            DMA((40,)), DMA((4,)), DMA((16,)), DMA((16,)), DMA((1,)), DMA,
        ],
        compiler_params=params(2),
        name="scatter_grads",
    )(stride_offset, wt, gpick.reshape(4, 16, 2, BLK, DH), gnear)
    return layer_out, grad_queries, gk, gv, gw


def solution(mesh):
    return jax.shard_map(
        body,
        mesh=mesh,
        in_specs=(P("ctx", "head"), P("ctx", "head"), P("ctx", "head"), P("head"),
                  P("head", None), P("ctx", "head")),
        out_specs=(P("ctx", "head"), P("ctx", "head"), P("ctx", "head"), P("ctx", "head"),
                   P("head", "ctx")),
        check_vma=False,
    )
```

```python
import jax
import jax.numpy as jnp
from jax import lax
from jax.experimental import pallas as pl
from jax.experimental.pallas import tpu as pltpu
from jax.sharding import PartitionSpec as P

T = 512
DH = 128
BLK = 64
NH = 8
NC = 32
SCALE = DH ** -0.5
EXP2_SCALE = SCALE * 1.4426950408889634
NEG = -1e30
MESH = pl.DeviceIdType.MESH
BF = jnp.bfloat16
F32 = jnp.float32


def where_am_i():
    c = lax.axis_index("ctx")
    h = lax.axis_index("head")
    return c, h, c // 4, (c // 2) % 2, c % 2


def ctx_id(z, yh, core):
    return z * 4 + yh * 2 + core


def across(h):
    return h + 1 - 2 * lax.rem(h, 2)


def head_peers(h):
    return lax.rem(h + 2, NH), lax.rem(h + NH - 2, NH), across(h)


def signal(barrier, c, h):
    pl.semaphore_signal(barrier, inc=1, device_id=(c, h), device_id_type=MESH)


class Sends:
    def __init__(self, sems):
        self.sems, self.made = sems, []

    def start(self, src, dst, recv, c, h):
        copy = pltpu.make_async_remote_copy(
            src_ref=src, dst_ref=dst, send_sem=self.sems.at[len(self.made)],
            recv_sem=recv, device_id=(c, h), device_id_type=MESH)
        copy.start()
        self.made.append(copy)

    def finish(self):
        for copy in self.made:
            copy.wait_send()


def arrived(ref, recv, send, c, h):
    pltpu.make_async_remote_copy(
        src_ref=ref, dst_ref=ref, send_sem=send, recv_sem=recv,
        device_id=(c, h), device_id_type=MESH).wait_recv()


def fold(x, op):
    return op(x.reshape(T // 8, 8, T), axis=0)


def nt(a, b):
    return lax.dot_general(a, b, (((1,), (1,)), ((), ())), preferred_element_type=F32)


def tn(a, b):
    return lax.dot_general(a, b, (((0,), (0,)), ((), ())), preferred_element_type=F32)


def nn(a, b):
    return jnp.dot(a, b, preferred_element_type=F32)


def step_kernel(off_ref, q_ref, k_ref, v_ref, g_ref, w_ref,
                lo_ref, gq_ref, gk_ref, gv_ref, gw_ref,
                picked, near, fg, att_all, wc, gpick, gnear,
                qs, scores, probs, dnear, top, inv, acc, dog, gatt,
                wts, pair_w, wup, wdown, wdone, wslot,
                pair_p, mine, up, down, done, yslot, brecv, csum, crecv,
                send, pk_recv, g_recv, c_recv, b_recv, w_recv, a_recv,
                pw_recv, wup_recv, wdown_recv, pp_recv, up_recv, down_recv,
                y_recv, near_recv, local):
    c, h, z, yh, core = where_am_i()
    partner = c + 1 - 2 * core
    ypeer = ctx_id(z, 1 - yh, core)
    after, before = lax.rem(c + 2, NC), lax.rem(c + NC - 2, NC)
    above = ctx_id(lax.rem(z + 1, 8), yh, core)
    below = ctx_id(lax.rem(z + 7, 8), yh, core)
    east, west, side = head_peers(h)
    west_side, east_side, far = across(west), across(east), head_peers(east)[0]
    far_side = across(far)
    hs = [lax.rem(h + d, NH) for d in range(1, NH)]
    barrier = pltpu.get_barrier_semaphore()

    def owner(d, y):
        return ctx_id(lax.rem(z + d, 8), lax.rem(yh + y, 2), core)

    for peer in (partner, ypeer, after, before, above, below):
        signal(barrier, peer, h)
    for peer in hs:
        signal(barrier, c, peer)
    for r in range(2):
        wanted = jnp.full((BLK, DH), 7 - off_ref[r], jnp.int32)
        for source, slot in ((k_ref, r), (v_ref, 2 + r)):
            rows = source[:BLK].astype(F32)
            for b in range(1, 8):
                rows = jnp.where(wanted == b, source[b * BLK:(b + 1) * BLK].astype(F32), rows)
            picked[slot, c] = rows.astype(BF)
    copies = [
        pltpu.make_async_copy(k_ref, near.at[0, 0], local.at[0]),
        pltpu.make_async_copy(v_ref, near.at[1, 0], local.at[1]),
        pltpu.make_async_copy(g_ref, fg.at[h], local.at[2]),
        pltpu.make_async_copy(
            w_ref.at[:, pl.ds(pl.multiple_of(h * T, T), T)],
            wc.at[pl.ds(pl.multiple_of(h * 256, 256), 256), :], local.at[3]),
    ]
    for copy in copies:
        copy.start()
    for r in range(2):
        qs[r] = q_ref[:, r * DH:(r + 1) * DH]
    dnear[...] = jnp.zeros_like(dnear)
    pl.semaphore_wait(barrier, 13)

    sends = Sends(send)

    def block(t):
        return picked.at[:, t]

    def pass_on(t, *peers):
        for peer in peers:
            sends.start(block(t), block(t), pk_recv.at[t], peer, h)

    def take(t, peer):
        arrived(block(t), pk_recv.at[t], send.at[0], peer, h)

    def gpart(n, half):
        return fg.at[n, pl.ds(half * 256, 256)]

    def own_part(half, peer):
        sends.start(g_ref.at[pl.ds(half * 256, 256)], gpart(h, half), g_recv.at[h, half], c, peer)

    def grelay(n, half, source, *peers):
        arrived(gpart(n, half), g_recv.at[n, half], send.at[0], c, source)
        for peer in peers:
            sends.start(gpart(n, half), gpart(n, half), g_recv.at[n, half], c, peer)

    def pick_ring(step):
        for y in range(2):
            t = owner(8 - step, y)
            take(t, below)
            pass_on(t, *((above, partner) if step < 4 else (partner,)))
            if step < 4:
                t = owner(step, y)
                take(t, above)
                pass_on(t, *((below, partner) if step < 3 else (partner,)))

    pass_on(c, ypeer, above, below, partner)
    own_part(0, east)
    own_part(1, west)
    own_part(0, side)
    sends.start(k_ref, near.at[0, 2], c_recv.at[0], after, h)
    sends.start(v_ref, near.at[1, 2], c_recv.at[1], after, h)
    own_part(1, east)
    own_part(0, west)
    own_part(1, side)
    take(ypeer, ypeer)
    pass_on(ypeer, above, below, partner)
    pick_ring(1)
    grelay(side, 0, side, east, west)
    grelay(west, 0, west, east)
    grelay(east, 1, east, west)
    pick_ring(2)
    pick_ring(3)
    grelay(side, 1, side, west, east)
    pick_ring(4)
    for n in range(2):
        arrived(near.at[n, 2], c_recv.at[n], send.at[0], before, h)
    for copy in copies:
        copy.wait()
    for n in range(2):
        sends.start(near.at[n, 2 * core], near.at[n, 1], b_recv.at[n], partner, h)
    grelay(west_side, 0, west, east)
    grelay(east_side, 1, east, west)
    flip = 1 - 2 * core
    for d in range(8):
        for y in range(2):
            t = owner(d, y) + flip
            take(t, partner)
    for n in range(2):
        arrived(near.at[n, 1], b_recv.at[n], send.at[0], partner, h)

    def tile(p):
        return pl.ds(pl.multiple_of(p * 8, 8), 8)

    def forward(r):
        q = qs[r]
        key = lax.broadcasted_iota(jnp.int32, (T, T), 0)
        query = lax.broadcasted_iota(jnp.int32, (T, T), 1)
        s = jnp.where(key <= query, nt(near[0, 0], q), NEG)
        scores[0] = s
        top[...] = fold(s, jnp.max)
        s = jnp.where(c >= 1, nt(near[0, 1], q), NEG)
        scores[1] = s
        top[...] = jnp.maximum(top[...], fold(s, jnp.max))
        kb, qb = key // BLK, query // BLK
        ok = ((kb > qb) | (kb == 7 - off_ref[r])) & (c >= 2)
        s = jnp.where(ok, nt(near[0, 2], q), NEG)
        scores[2] = s
        top[...] = jnp.maximum(top[...], fold(s, jnp.max))

        def pick_scores(p, _):
            rows = lax.broadcasted_iota(jnp.int32, (T, T), 0)
            s = nt(picked[r, tile(p)].reshape(T, DH), q)
            s = jnp.where(rows < (c - 2) * BLK - p * T, s, NEG)
            scores[3 + p] = s
            top[...] = jnp.maximum(top[...], fold(s, jnp.max))
            return 0

        lax.fori_loop(0, 4, pick_scores, 0)
        m = jnp.max(top[...], axis=0, keepdims=True)
        top[...] = jnp.zeros_like(top)
        acc[...] = jnp.zeros_like(acc)

        def weigh(i, values):
            w = jnp.exp2((scores[i] - m) * EXP2_SCALE)
            top[...] += fold(w, jnp.sum)
            w = w.astype(BF)
            probs[r, i] = w
            acc[...] += tn(values, w)

        def near_mix(i, _):
            weigh(i, near[1, i])
            return 0

        def pick_mix(p, _):
            weigh(3 + p, picked[2 + r, tile(p)].reshape(T, DH))
            return 0

        lax.fori_loop(0, 3, near_mix, 0)
        lax.fori_loop(0, 4, pick_mix, 0)
        total = 1.0 / jnp.sum(top[...], axis=0, keepdims=True)
        inv[r] = jnp.broadcast_to(total, (8, T))
        att_all[h, pl.ds(r * DH, DH), :] = (acc[...] * total).astype(BF)

    def part(n, half):
        return att_all.at[n, pl.ds(half * DH, DH)]

    def relay(n, half, source, *peers):
        if source is not None:
            arrived(part(n, half), a_recv.at[n, half], send.at[0], c, source)
        for peer in peers:
            sends.start(part(n, half), part(n, half), a_recv.at[n, half], c, peer)

    def piece(half, r):
        return wc.at[pl.ds(pl.multiple_of(r * 256, 256), 256),
                     pl.ds(pl.multiple_of(half * 256, 256), 256)]

    forward(0)
    relay(h, 0, None, east, side, west)
    forward(1)
    relay(h, 1, None, west, side, east)
    for n, half, source in (
            (west, 1, west), (east, 0, east), (west_side, 1, west), (east_side, 0, east),
            (far, 0, west), (far, 1, east), (far_side, 0, west), (far_side, 1, east)):
        grelay(n, half, source)

    order = [lax.rem(z + d, 8) for d in (4, 5, 3, 6, 2, 7, 1, 0)]
    for t in order:
        term = nn(att_all[h], fg[t])
        for j in range(4):
            wts[t, j % 2, j // 2] = term[:, j * DH:(j + 1) * DH].astype(BF)
        sends.start(wts.at[t, 1 - core], pair_w.at[t], pw_recv.at[t], partner, h)

    def quad(p):
        return pl.ds(pl.multiple_of(p * 4, 4), 4)

    def combine(t):
        arrived(pair_w.at[t], pw_recv.at[t], send.at[0], partner, h)
        wts[t, core] = (wts[t, core].astype(F32) + pair_w[t].astype(F32)).astype(BF)

    def grads(r, i, keys, values, rowdot):
        w = probs[r, i]
        do = dog[...]
        dp = nt(values, do)
        ds = (w.astype(F32) * (dp - rowdot)).astype(BF)
        acc[...] += tn(keys, ds)
        return nn(ds, qs[r]) * SCALE, nn(w, do)

    def start_backward(r):
        rows = pl.ds(r * DH, DH)
        grad = gatt[rows, :].astype(BF).astype(F32)
        total = inv[r, 0:1]
        dog[...] = (grad * total).T.astype(BF)
        acc[...] = jnp.zeros_like(acc)
        return jnp.sum(grad * att_all[h, rows, :].astype(F32), axis=0, keepdims=True) * total

    def backward_near(r, rowdot):
        def near_grads(i, _):
            dk, dv = grads(r, i, near[0, i], near[1, i], rowdot)
            dnear[0, i] += dk
            dnear[1, i] += dv
            return 0

        lax.fori_loop(0, 3, near_grads, 0)

    def backward_pick(r, rowdot):
        def pick_grads(p, _):
            dk, dv = grads(r, 3 + p, picked[r, tile(p)].reshape(T, DH),
                           picked[2 + r, tile(p)].reshape(T, DH), rowdot)
            gpick[r, 0, quad(p)] = dk.astype(BF).reshape(4, 2, BLK, DH)
            gpick[r, 1, quad(p)] = dv.astype(BF).reshape(4, 2, BLK, DH)
            return 0

        lax.fori_loop(0, 4, pick_grads, 0)
        gq_ref[:, r * DH:(r + 1) * DH] = (acc[...].T * SCALE).astype(BF)

    def w_ring(step):
        t = order[2 + 2 * step]
        combine(t)
        arrived(wup.at[step], wup_recv.at[step], send.at[0], below, h)
        wup[step] = (wup[step].astype(F32) + wts[t, core].astype(F32)).astype(BF)
        sends.start(wup.at[step], wup.at[step + 1], wup_recv.at[step + 1], above, h)
        t = order[3 + 2 * step]
        combine(t)
        if step < 2:
            arrived(wdown.at[step], wdown_recv.at[step], send.at[0], above, h)
            wdown[step] = (wdown[step].astype(F32) + wts[t, core].astype(F32)).astype(BF)
            sends.start(wdown.at[step], wdown.at[step + 1], wdown_recv.at[step + 1], below, h)

    def pair(t):
        return pl.ds(pl.multiple_of(t * 2, 2), 2)

    def share_picks(r):
        for t in order:
            sends.start(gpick.at[r, :, pair(t), 1 - core], pair_p.at[r, t], pp_recv.at[r, t],
                        partner, h)

    def combine_picks(r, t):
        arrived(pair_p.at[r, t], pp_recv.at[r, t], send.at[0], partner, h)
        for y in range(2):
            own = gpick[r, :, t * 2 + y, core].astype(F32) + pair_p[r, t, :, y].astype(F32)
            mine[r, t, y] = own.astype(BF).reshape(DH, DH)

    def open_ring(r):
        combine_picks(r, order[0])
        sends.start(mine.at[r, order[0]], up.at[r, 0], up_recv.at[r, 0], above, h)
        combine_picks(r, order[1])
        sends.start(mine.at[r, order[1]], down.at[r, 0], down_recv.at[r, 0], below, h)

    def sum_ring(r, step):
        t = order[2 + 2 * step]
        combine_picks(r, t)
        arrived(up.at[r, step], up_recv.at[r, step], send.at[0], below, h)
        up[r, step] = (up[r, step].astype(F32) + mine[r, t].astype(F32)).astype(BF)
        sends.start(up.at[r, step], up.at[r, step + 1], up_recv.at[r, step + 1], above, h)
        t = order[3 + 2 * step]
        combine_picks(r, t)
        if step < 2:
            arrived(down.at[r, step], down_recv.at[r, step], send.at[0], above, h)
            down[r, step] = (down[r, step].astype(F32) + mine[r, t].astype(F32)).astype(BF)
            sends.start(down.at[r, step], down.at[r, step + 1], down_recv.at[r, step + 1],
                        below, h)

    def close_ring(r):
        arrived(down.at[r, 2], down_recv.at[r, 2], send.at[0], above, h)
        arrived(up.at[r, 3], up_recv.at[r, 3], send.at[0], below, h)
        done[r] = (mine[r, z].astype(F32) + up[r, 3].astype(F32)
                   + down[r, 2].astype(F32)).astype(BF)
        sends.start(done.at[r, 1 - yh], yslot.at[r], y_recv.at[r], ypeer, h)

    gatt[...] = jnp.zeros_like(gatt)

    def grad_att(r, _):
        gatt[...] += nt(w_ref[:, pl.ds(pl.multiple_of(r * T, T), T)], fg[r])
        return 0

    lax.fori_loop(0, NH, grad_att, 0)
    rowdot = start_backward(0)
    relay(side, 0, side, east, west)
    relay(west, 0, west, east)
    combine(order[0])
    sends.start(wts.at[order[0], core], wup.at[0], wup_recv.at[0], above, h)
    combine(order[1])
    sends.start(wts.at[order[1], core], wdown.at[0], wdown_recv.at[0], below, h)
    backward_near(0, rowdot)
    relay(side, 1, side, west, east)
    relay(east, 1, east, west)
    w_ring(0)
    for peer in hs:
        sends.start(w_ref.at[:, pl.ds(pl.multiple_of(peer * T + core * 256, 256), 256)],
                    piece(core, h), w_recv.at[core, h], c, peer)
    backward_pick(0, rowdot)
    share_picks(0)
    relay(west_side, 0, west, east)
    relay(east_side, 1, east, west)
    w_ring(1)
    rowdot = start_backward(1)
    backward_near(1, rowdot)
    gnear[...] = dnear[...].astype(BF)
    sends.start(gnear.at[:, 1], brecv, near_recv.at[0], partner, h)
    w_ring(2)
    open_ring(0)
    backward_pick(1, rowdot)
    share_picks(1)
    sum_ring(0, 0)
    arrived(wdown.at[2], wdown_recv.at[2], send.at[0], above, h)
    arrived(wup.at[3], wup_recv.at[3], send.at[0], below, h)
    wdone[...] = (wts[z, core].astype(F32) + wup[3].astype(F32)
                  + wdown[2].astype(F32)).astype(BF)
    sends.start(wdone.at[1 - yh], wslot, y_recv.at[2], ypeer, h)
    open_ring(1)
    arrived(brecv, near_recv.at[0], send.at[0], partner, h)
    extra = brecv[...].astype(F32)
    csum[...] = (gnear[:, 2].astype(F32) + jnp.where(core == 1, extra, 0.0)).astype(BF)
    sends.start(csum, crecv, near_recv.at[1], before, h)
    sum_ring(0, 1)
    for peer in hs:
        arrived(piece(core, peer), w_recv.at[core, peer], send.at[0], c, peer)
        sends.start(piece(core, peer), piece(core, peer), w_recv.at[core, peer], partner, h)
    sum_ring(1, 0)
    sum_ring(0, 2)
    relay(west, 1, west)
    relay(east, 0, east)
    relay(west_side, 1, west)
    relay(east_side, 0, east)
    relay(far, 0, west)
    relay(far, 1, east)
    relay(far_side, 0, west)
    relay(far_side, 1, east)
    sum_ring(1, 1)
    close_ring(0)
    for peer in hs:
        arrived(piece(1 - core, peer), w_recv.at[1 - core, peer], send.at[0], partner, h)
    scores[0] = jnp.zeros((T, T), F32)

    def project(r, _):
        scores[0] += tn(att_all[r], wc[pl.ds(pl.multiple_of(r * 256, 256), 256), :])
        return 0

    lax.fori_loop(0, 4, project, 0)
    sum_ring(1, 2)
    lax.fori_loop(4, NH, project, 0)
    close_ring(1)
    lo_ref[...] = scores[0].astype(BF)
    arrived(wslot, y_recv.at[2], send.at[0], ypeer, h)
    gw_ref[...] = (wdone[yh].astype(F32) + wslot[...].astype(F32)).astype(BF)
    arrived(crecv, near_recv.at[1], send.at[0], after, h)
    grad = gnear[:, 0].astype(F32) + jnp.where(core == 1, 0.0, extra) + crecv[...].astype(F32)
    block = lax.broadcasted_iota(jnp.int32, (T, DH), 0) // BLK
    grads_out = [grad[0], grad[1]]
    for r in range(2):
        arrived(yslot.at[r], y_recv.at[r], send.at[0], ypeer, h)
        total = done[r, yh].astype(F32) + yslot[r].astype(F32)
        for n in range(2):
            spread = jnp.concatenate([total[n * BLK:(n + 1) * BLK]] * 8, axis=0)
            grads_out[n] += jnp.where(block == 7 - off_ref[r], spread, 0.0)
    gk_ref[...] = grads_out[0].astype(BF)
    gv_ref[...] = grads_out[1].astype(BF)
    sends.finish()


def hand_over(*refs):
    for source, target in zip(refs[:5], refs[5:]):
        target[...] = source[...]


VM = pl.BlockSpec(memory_space=pltpu.VMEM)
SM = pl.BlockSpec(memory_space=pltpu.SMEM)
DMA = pltpu.SemaphoreType.DMA


def shaped(*shape, dtype=BF):
    return jax.ShapeDtypeStruct(shape, dtype)


def params(number):
    return pltpu.CompilerParams(
        collective_id=number, has_side_effects=True, vmem_limit_bytes=60 << 20)


def buf(*shape, dtype=BF):
    return pltpu.VMEM(shape, dtype)


def body(queries, keys, values, stride_offset, w_out, grad_out):
    shapes = (shaped(T, T), shaped(T, 256), shaped(T, DH), shaped(T, DH), shaped(256, DH))
    results = pl.pallas_call(
        step_kernel,
        out_shape=shapes,
        in_specs=[SM, VM, VM, VM, VM, VM],
        out_specs=(VM,) * 5,
        scratch_shapes=[
            buf(4, NC, BLK, DH), buf(2, 3, T, DH), buf(NH, T, T), buf(NH, 256, T),
            buf(2048, T), buf(2, 2, 16, 2, BLK, DH), buf(2, 3, T, DH),
            buf(2, T, DH), buf(7, T, T, dtype=F32), buf(2, 7, T, T),
            buf(2, 3, T, DH, dtype=F32), buf(8, T, dtype=F32), buf(2, 8, T, dtype=F32),
            buf(DH, T, dtype=F32), buf(T, DH), buf(256, T, dtype=F32),
            buf(8, 2, 2, 256, DH), buf(8, 2, 256, DH), buf(4, 2, 256, DH), buf(3, 2, 256, DH),
            buf(2, 256, DH), buf(256, DH),
            buf(2, 8, 2, 2, BLK, DH), buf(2, 8, 2, DH, DH), buf(2, 4, 2, DH, DH),
            buf(2, 3, 2, DH, DH), buf(2, 2, DH, DH), buf(2, DH, DH),
            buf(2, T, DH), buf(2, T, DH), buf(2, T, DH),
            DMA((140,)), DMA((NC,)), DMA((NH, 2)), DMA((2,)), DMA((2,)), DMA((2, NH)),
            DMA((NH, 2)), DMA((8,)), DMA((4,)), DMA((3,)), DMA((2, 8)), DMA((2, 4)),
            DMA((2, 3)), DMA((3,)), DMA((2,)), DMA((4,)),
        ],
        compiler_params=params(0),
        name="step",
    )(stride_offset, queries, keys, values, grad_out, w_out)
    return pl.pallas_call(
        hand_over, out_shape=shapes, in_specs=[VM] * 5, out_specs=(VM,) * 5, name="hand_over",
    )(*results)


def solution(mesh):
    return jax.shard_map(
        body,
        mesh=mesh,
        in_specs=(P("ctx", "head"), P("ctx", "head"), P("ctx", "head"), P("head"),
                  P("head", None), P("ctx", "head")),
        out_specs=(P("ctx", "head"), P("ctx", "head"), P("ctx", "head"), P("ctx", "head"),
                   P("head", "ctx")),
        check_vma=False,
    )
```

```python
import jax
import jax.numpy as jnp
from jax import lax
from jax.experimental import pallas as pl
from jax.experimental.pallas import tpu as pltpu
from jax.sharding import PartitionSpec as P

T = 512
DH = 128
BLK = 64
NH = 8
NC = 32
SCALE = DH ** -0.5
EXP2_SCALE = SCALE * 1.4426950408889634
NEG = -1e30
MESH = pl.DeviceIdType.MESH
BF = jnp.bfloat16
F32 = jnp.float32


def where_am_i():
    c = lax.axis_index("ctx")
    h = lax.axis_index("head")
    return c, h, c // 4, (c // 2) % 2, c % 2


def ctx_id(z, yh, core):
    return z * 4 + yh * 2 + core


def across(h):
    return h + 1 - 2 * lax.rem(h, 2)


def head_peers(h):
    return lax.rem(h + 2, NH), lax.rem(h + NH - 2, NH), across(h)


def signal(barrier, c, h):
    pl.semaphore_signal(barrier, inc=1, device_id=(c, h), device_id_type=MESH)


class Sends:
    def __init__(self, sems):
        self.sems, self.made = sems, []

    def start(self, src, dst, recv, c, h):
        copy = pltpu.make_async_remote_copy(
            src_ref=src, dst_ref=dst, send_sem=self.sems.at[len(self.made)],
            recv_sem=recv, device_id=(c, h), device_id_type=MESH)
        copy.start()
        self.made.append(copy)

    def finish(self):
        for copy in self.made:
            copy.wait_send()


def arrived(ref, recv, send, c, h):
    pltpu.make_async_remote_copy(
        src_ref=ref, dst_ref=ref, send_sem=send, recv_sem=recv,
        device_id=(c, h), device_id_type=MESH).wait_recv()


def fold(x, op):
    return op(x.reshape(T // 8, 8, T), axis=0)


def nt(a, b):
    return lax.dot_general(a, b, (((1,), (1,)), ((), ())), preferred_element_type=F32)


def tn(a, b):
    return lax.dot_general(a, b, (((0,), (0,)), ((), ())), preferred_element_type=F32)


def nn(a, b):
    return jnp.dot(a, b, preferred_element_type=F32)


def step_kernel(off_ref, q_ref, k_ref, v_ref, g_ref, w_ref,
                lo_ref, gq_ref, gk_ref, gv_ref, gw_ref,
                picked, near, fg, att_all, wc, gpick, gnear,
                qs, scores, probs, dnear, top, inv, acc, dog, gatt, rdot,
                wts, pair_w, wup, wdown, wdone, wslot,
                pair_p, mine, up, down, done, yslot, brecv, csum, crecv,
                send, pk_recv, g_recv, c_recv, b_recv, w_recv, a_recv,
                pw_recv, wup_recv, wdown_recv, pp_recv, up_recv, down_recv,
                y_recv, near_recv, local):
    c, h, z, yh, core = where_am_i()
    partner = c + 1 - 2 * core
    ypeer = ctx_id(z, 1 - yh, core)
    after, before = lax.rem(c + 2, NC), lax.rem(c + NC - 2, NC)
    above = ctx_id(lax.rem(z + 1, 8), yh, core)
    below = ctx_id(lax.rem(z + 7, 8), yh, core)
    east, west, side = head_peers(h)
    west_side, east_side, far = across(west), across(east), head_peers(east)[0]
    far_side = across(far)
    hs = [lax.rem(h + d, NH) for d in range(1, NH)]
    barrier = pltpu.get_barrier_semaphore()

    def owner(d, y):
        return ctx_id(lax.rem(z + d, 8), lax.rem(yh + y, 2), core)

    for peer in (partner, ypeer, after, before, above, below):
        signal(barrier, peer, h)
    for peer in hs:
        signal(barrier, c, peer)
    for r in range(2):
        wanted = jnp.full((BLK, DH), 7 - off_ref[r], jnp.int32)
        for source, slot in ((k_ref, r), (v_ref, 2 + r)):
            rows = source[:BLK].astype(F32)
            for b in range(1, 8):
                rows = jnp.where(wanted == b, source[b * BLK:(b + 1) * BLK].astype(F32), rows)
            picked[slot, c] = rows.astype(BF)
    copies = [
        pltpu.make_async_copy(k_ref, near.at[0, 0], local.at[0]),
        pltpu.make_async_copy(v_ref, near.at[1, 0], local.at[1]),
        pltpu.make_async_copy(g_ref, fg.at[h], local.at[2]),
        pltpu.make_async_copy(
            w_ref.at[:, pl.ds(pl.multiple_of(h * T, T), T)],
            wc.at[pl.ds(pl.multiple_of(h * 256, 256), 256), :], local.at[3]),
    ]
    for copy in copies:
        copy.start()
    for r in range(2):
        qs[r] = q_ref[:, r * DH:(r + 1) * DH]
    dnear[...] = jnp.zeros_like(dnear)
    def tile(p):
        return pl.ds(pl.multiple_of(p * 8, 8), 8)

    def own_scores(r):
        key = lax.broadcasted_iota(jnp.int32, (T, T), 0)
        query = lax.broadcasted_iota(jnp.int32, (T, T), 1)
        s = jnp.where(key <= query, nt(k_ref[...], qs[r]), NEG)
        scores[r, 0] = s
        top[r] = fold(s, jnp.max)

    def last_scores(r):
        s = jnp.where(c >= 1, nt(near[0, 1], qs[r]), NEG)
        scores[r, 1] = s
        top[r] = jnp.maximum(top[r], fold(s, jnp.max))

    def edge_scores(r):
        kb = lax.broadcasted_iota(jnp.int32, (T, T), 0) // BLK
        qb = lax.broadcasted_iota(jnp.int32, (T, T), 1) // BLK
        ok = ((kb > qb) | (kb == 7 - off_ref[r])) & (c >= 2)
        s = jnp.where(ok, nt(near[0, 2], qs[r]), NEG)
        scores[r, 2] = s
        top[r] = jnp.maximum(top[r], fold(s, jnp.max))

    def forward(r):
        def pick_scores(p, _):
            rows = lax.broadcasted_iota(jnp.int32, (T, T), 0)
            s = nt(picked[r, tile(p)].reshape(T, DH), qs[r])
            s = jnp.where(rows < (c - 2) * BLK - p * T, s, NEG)
            scores[r, 3 + p] = s
            top[r] = jnp.maximum(top[r], fold(s, jnp.max))
            return 0

        lax.fori_loop(0, 4, pick_scores, 0)
        m = jnp.max(top[r], axis=0, keepdims=True)
        top[r] = jnp.zeros((8, T), F32)
        acc[r] = jnp.zeros((DH, T), F32)

        def weigh(i, values):
            w = jnp.exp2((scores[r, i] - m) * EXP2_SCALE)
            top[r] += fold(w, jnp.sum)
            w = w.astype(BF)
            probs[r, i] = w
            acc[r] += tn(values, w)

        def near_mix(i, _):
            weigh(i, near[1, i])
            return 0

        def pick_mix(p, _):
            weigh(3 + p, picked[2 + r, tile(p)].reshape(T, DH))
            return 0

        lax.fori_loop(0, 3, near_mix, 0)
        lax.fori_loop(0, 4, pick_mix, 0)
        total = 1.0 / jnp.sum(top[r], axis=0, keepdims=True)
        inv[r] = jnp.broadcast_to(total, (8, T))
        att_all[h, pl.ds(r * DH, DH), :] = (acc[r] * total).astype(BF)

    def grad_att(r, block):
        gatt[...] += nt(w_ref[:, pl.ds(pl.multiple_of(r * T, T), T)], block)

    own_scores(0)
    own_scores(1)
    gatt[...] = jnp.zeros_like(gatt)
    grad_att(h, g_ref[...])
    pl.semaphore_wait(barrier, 13)

    sends = Sends(send)

    def block(t):
        return picked.at[:, t]

    def pass_on(t, *peers):
        for peer in peers:
            sends.start(block(t), block(t), pk_recv.at[t], peer, h)

    def take(t, peer):
        arrived(block(t), pk_recv.at[t], send.at[0], peer, h)

    def gpart(n, half):
        return fg.at[n, pl.ds(half * 256, 256)]

    def own_part(half, peer):
        sends.start(g_ref.at[pl.ds(half * 256, 256)], gpart(h, half), g_recv.at[h, half], c, peer)

    def grelay(n, half, source, *peers):
        arrived(gpart(n, half), g_recv.at[n, half], send.at[0], c, source)
        for peer in peers:
            sends.start(gpart(n, half), gpart(n, half), g_recv.at[n, half], c, peer)

    def pick_ring(step):
        for y in range(2):
            t = owner(8 - step, y)
            take(t, below)
            pass_on(t, *((above, partner) if step < 4 else (partner,)))
            if step < 4:
                t = owner(step, y)
                take(t, above)
                pass_on(t, *((below, partner) if step < 3 else (partner,)))

    pass_on(c, ypeer, above, below, partner)
    own_part(0, east)
    own_part(1, west)
    own_part(0, side)
    sends.start(k_ref, near.at[0, 2], c_recv.at[0], after, h)
    sends.start(v_ref, near.at[1, 2], c_recv.at[1], after, h)
    own_part(1, east)
    own_part(0, west)
    own_part(1, side)
    take(ypeer, ypeer)
    pass_on(ypeer, above, below, partner)
    pick_ring(1)
    grelay(side, 0, side, east, west)
    grelay(west, 0, west, east)
    grelay(east, 1, east, west)
    pick_ring(2)
    for n in range(2):
        arrived(near.at[n, 2], c_recv.at[n], send.at[0], before, h)
    for copy in copies:
        copy.wait()
    for n in range(2):
        sends.start(near.at[n, 2 * core], near.at[n, 1], b_recv.at[n], partner, h)
    edge_scores(0)
    pick_ring(3)
    edge_scores(1)
    grelay(side, 1, side, west, east)
    grad_att(side, fg[side])
    pick_ring(4)
    grelay(west_side, 0, west, east)
    grelay(east_side, 1, east, west)
    flip = 1 - 2 * core
    for n in range(2):
        arrived(near.at[n, 1], b_recv.at[n], send.at[0], partner, h)
    last_scores(0)
    last_scores(1)
    for d in range(8):
        for y in range(2):
            t = owner(d, y) + flip
            take(t, partner)

    def part(n, half):
        return att_all.at[n, pl.ds(half * DH, DH)]

    def relay(n, half, source, *peers):
        if source is not None:
            arrived(part(n, half), a_recv.at[n, half], send.at[0], c, source)
        for peer in peers:
            sends.start(part(n, half), part(n, half), a_recv.at[n, half], c, peer)

    def piece(half, r):
        return wc.at[pl.ds(pl.multiple_of(r * 256, 256), 256),
                     pl.ds(pl.multiple_of(half * 256, 256), 256)]

    forward(0)
    relay(h, 0, None, east, side, west)
    forward(1)
    relay(h, 1, None, west, side, east)
    for n, half, source in (
            (west, 1, west), (east, 0, east), (west_side, 1, west), (east_side, 0, east),
            (far, 0, west), (far, 1, east), (far_side, 0, west), (far_side, 1, east)):
        grelay(n, half, source)
    for n in (west, east, west_side, east_side, far, far_side):
        grad_att(n, fg[n])

    order = [lax.rem(z + d, 8) for d in (4, 5, 3, 6, 2, 7, 1, 0)]
    for t in order:
        term = nn(att_all[h], fg[t])
        for j in range(4):
            wts[t, j % 2, j // 2] = term[:, j * DH:(j + 1) * DH].astype(BF)
        sends.start(wts.at[t, 1 - core], pair_w.at[t], pw_recv.at[t], partner, h)

    def quad(p):
        return pl.ds(pl.multiple_of(p * 4, 4), 4)

    def combine(t):
        arrived(pair_w.at[t], pw_recv.at[t], send.at[0], partner, h)
        wts[t, core] = (wts[t, core].astype(F32) + pair_w[t].astype(F32)).astype(BF)

    def grads(r, i, keys, values):
        w = probs[r, i]
        do = dog[r]
        dp = nt(values, do)
        ds = (w.astype(F32) * (dp - rdot[r, 0:1])).astype(BF)
        acc[r] += tn(keys, ds)
        return nn(ds, qs[r]) * SCALE, nn(w, do)

    def start_backward(r):
        rows = pl.ds(r * DH, DH)
        grad = gatt[rows, :].astype(BF).astype(F32)
        total = inv[r, 0:1]
        dog[r] = (grad * total).T.astype(BF)
        acc[r] = jnp.zeros((DH, T), F32)
        rdot[r] = jnp.broadcast_to(
            jnp.sum(grad * att_all[h, rows, :].astype(F32), axis=0, keepdims=True) * total, (8, T))

    def backward_near(r, first, last):
        def near_grads(i, _):
            dk, dv = grads(r, i, near[0, i], near[1, i])
            dnear[0, i] += dk
            dnear[1, i] += dv
            return 0

        lax.fori_loop(first, last, near_grads, 0)

    def backward_pick(r):
        def pick_grads(p, _):
            dk, dv = grads(r, 3 + p, picked[r, tile(p)].reshape(T, DH),
                           picked[2 + r, tile(p)].reshape(T, DH))
            gpick[r, 0, quad(p)] = dk.astype(BF).reshape(4, 2, BLK, DH)
            gpick[r, 1, quad(p)] = dv.astype(BF).reshape(4, 2, BLK, DH)
            return 0

        lax.fori_loop(0, 4, pick_grads, 0)

    def w_ring(step):
        t = order[2 + 2 * step]
        combine(t)
        arrived(wup.at[step], wup_recv.at[step], send.at[0], below, h)
        wup[step] = (wup[step].astype(F32) + wts[t, core].astype(F32)).astype(BF)
        sends.start(wup.at[step], wup.at[step + 1], wup_recv.at[step + 1], above, h)
        t = order[3 + 2 * step]
        combine(t)
        if step < 2:
            arrived(wdown.at[step], wdown_recv.at[step], send.at[0], above, h)
            wdown[step] = (wdown[step].astype(F32) + wts[t, core].astype(F32)).astype(BF)
            sends.start(wdown.at[step], wdown.at[step + 1], wdown_recv.at[step + 1], below, h)

    def pair(t):
        return pl.ds(pl.multiple_of(t * 2, 2), 2)

    def share_picks(r):
        for t in order:
            sends.start(gpick.at[r, :, pair(t), 1 - core], pair_p.at[r, t], pp_recv.at[r, t],
                        partner, h)

    def combine_picks(r, t):
        arrived(pair_p.at[r, t], pp_recv.at[r, t], send.at[0], partner, h)
        for y in range(2):
            own = gpick[r, :, t * 2 + y, core].astype(F32) + pair_p[r, t, :, y].astype(F32)
            mine[r, t, y] = own.astype(BF).reshape(DH, DH)

    def open_ring(r):
        combine_picks(r, order[0])
        sends.start(mine.at[r, order[0]], up.at[r, 0], up_recv.at[r, 0], above, h)
        combine_picks(r, order[1])
        sends.start(mine.at[r, order[1]], down.at[r, 0], down_recv.at[r, 0], below, h)

    def sum_ring(r, step):
        t = order[2 + 2 * step]
        combine_picks(r, t)
        arrived(up.at[r, step], up_recv.at[r, step], send.at[0], below, h)
        up[r, step] = (up[r, step].astype(F32) + mine[r, t].astype(F32)).astype(BF)
        sends.start(up.at[r, step], up.at[r, step + 1], up_recv.at[r, step + 1], above, h)
        t = order[3 + 2 * step]
        combine_picks(r, t)
        if step < 2:
            arrived(down.at[r, step], down_recv.at[r, step], send.at[0], above, h)
            down[r, step] = (down[r, step].astype(F32) + mine[r, t].astype(F32)).astype(BF)
            sends.start(down.at[r, step], down.at[r, step + 1], down_recv.at[r, step + 1],
                        below, h)

    def close_ring(r):
        arrived(down.at[r, 2], down_recv.at[r, 2], send.at[0], above, h)
        arrived(up.at[r, 3], up_recv.at[r, 3], send.at[0], below, h)
        done[r] = (mine[r, z].astype(F32) + up[r, 3].astype(F32)
                   + down[r, 2].astype(F32)).astype(BF)
        sends.start(done.at[r, 1 - yh], yslot.at[r], y_recv.at[r], ypeer, h)

    start_backward(0)
    relay(side, 0, side, east, west)
    relay(west, 0, west, east)
    combine(order[0])
    sends.start(wts.at[order[0], core], wup.at[0], wup_recv.at[0], above, h)
    combine(order[1])
    sends.start(wts.at[order[1], core], wdown.at[0], wdown_recv.at[0], below, h)
    backward_pick(0)
    share_picks(0)
    relay(side, 1, side, west, east)
    relay(east, 1, east, west)
    w_ring(0)
    for peer in hs:
        sends.start(w_ref.at[:, pl.ds(pl.multiple_of(peer * T + core * 256, 256), 256)],
                    piece(core, h), w_recv.at[core, h], c, peer)
    backward_near(0, 1, 3)
    relay(west_side, 0, west, east)
    relay(east_side, 1, east, west)
    w_ring(1)
    open_ring(0)
    start_backward(1)
    backward_pick(1)
    share_picks(1)
    w_ring(2)
    sum_ring(0, 0)
    backward_near(1, 1, 3)
    gnear[:, 1:] = dnear[:, 1:].astype(BF)
    sends.start(gnear.at[:, 1], brecv, near_recv.at[0], partner, h)
    open_ring(1)
    sum_ring(0, 1)
    backward_near(0, 0, 1)
    arrived(brecv, near_recv.at[0], send.at[0], partner, h)
    extra = brecv[...].astype(F32)
    csum[...] = (gnear[:, 2].astype(F32) + jnp.where(core == 1, extra, 0.0)).astype(BF)
    sends.start(csum, crecv, near_recv.at[1], before, h)
    backward_near(1, 0, 1)
    sum_ring(1, 0)
    arrived(wdown.at[2], wdown_recv.at[2], send.at[0], above, h)
    arrived(wup.at[3], wup_recv.at[3], send.at[0], below, h)
    wdone[...] = (wts[z, core].astype(F32) + wup[3].astype(F32)
                  + wdown[2].astype(F32)).astype(BF)
    sends.start(wdone.at[1 - yh], wslot, y_recv.at[2], ypeer, h)
    for peer in hs:
        arrived(piece(core, peer), w_recv.at[core, peer], send.at[0], c, peer)
        sends.start(piece(core, peer), piece(core, peer), w_recv.at[core, peer], partner, h)
    for r in range(2):
        gq_ref[:, r * DH:(r + 1) * DH] = (acc[r].T * SCALE).astype(BF)
    sum_ring(0, 2)
    relay(west, 1, west)
    relay(east, 0, east)
    relay(west_side, 1, west)
    relay(east_side, 0, east)
    relay(far, 0, west)
    relay(far, 1, east)
    relay(far_side, 0, west)
    relay(far_side, 1, east)
    sum_ring(1, 1)
    close_ring(0)
    for peer in hs:
        arrived(piece(1 - core, peer), w_recv.at[1 - core, peer], send.at[0], partner, h)
    scores[0, 0] = jnp.zeros((T, T), F32)

    def project(r, _):
        scores[0, 0] += tn(att_all[r], wc[pl.ds(pl.multiple_of(r * 256, 256), 256), :])
        return 0

    lax.fori_loop(0, 4, project, 0)
    sum_ring(1, 2)
    lax.fori_loop(4, NH, project, 0)
    close_ring(1)
    lo_ref[...] = scores[0, 0].astype(BF)
    arrived(wslot, y_recv.at[2], send.at[0], ypeer, h)
    gw_ref[...] = (wdone[yh].astype(F32) + wslot[...].astype(F32)).astype(BF)
    arrived(crecv, near_recv.at[1], send.at[0], after, h)
    grad = dnear[:, 0] + jnp.where(core == 1, 0.0, extra) + crecv[...].astype(F32)
    block = lax.broadcasted_iota(jnp.int32, (T, DH), 0) // BLK
    grads_out = [grad[0], grad[1]]
    for r in range(2):
        arrived(yslot.at[r], y_recv.at[r], send.at[0], ypeer, h)
        total = done[r, yh].astype(F32) + yslot[r].astype(F32)
        for n in range(2):
            spread = jnp.concatenate([total[n * BLK:(n + 1) * BLK]] * 8, axis=0)
            grads_out[n] += jnp.where(block == 7 - off_ref[r], spread, 0.0)
    gk_ref[...] = grads_out[0].astype(BF)
    gv_ref[...] = grads_out[1].astype(BF)
    sends.finish()


def hand_over(*refs):
    for source, target in zip(refs[:5], refs[5:]):
        target[...] = source[...]


VM = pl.BlockSpec(memory_space=pltpu.VMEM)
SM = pl.BlockSpec(memory_space=pltpu.SMEM)
DMA = pltpu.SemaphoreType.DMA


def shaped(*shape, dtype=BF):
    return jax.ShapeDtypeStruct(shape, dtype)


def params(number):
    return pltpu.CompilerParams(
        collective_id=number, has_side_effects=True, vmem_limit_bytes=60 << 20)


def buf(*shape, dtype=BF):
    return pltpu.VMEM(shape, dtype)


def body(queries, keys, values, stride_offset, w_out, grad_out):
    shapes = (shaped(T, T), shaped(T, 256), shaped(T, DH), shaped(T, DH), shaped(256, DH))
    results = pl.pallas_call(
        step_kernel,
        out_shape=shapes,
        in_specs=[SM, VM, VM, VM, VM, VM],
        out_specs=(VM,) * 5,
        scratch_shapes=[
            buf(4, NC, BLK, DH), buf(2, 3, T, DH), buf(NH, T, T), buf(NH, 256, T),
            buf(2048, T), buf(2, 2, 16, 2, BLK, DH), buf(2, 3, T, DH),
            buf(2, T, DH), buf(2, 7, T, T, dtype=F32), buf(2, 7, T, T),
            buf(2, 3, T, DH, dtype=F32), buf(2, 8, T, dtype=F32), buf(2, 8, T, dtype=F32),
            buf(2, DH, T, dtype=F32), buf(2, T, DH), buf(256, T, dtype=F32), buf(2, 8, T, dtype=F32),
            buf(8, 2, 2, 256, DH), buf(8, 2, 256, DH), buf(4, 2, 256, DH), buf(3, 2, 256, DH),
            buf(2, 256, DH), buf(256, DH),
            buf(2, 8, 2, 2, BLK, DH), buf(2, 8, 2, DH, DH), buf(2, 4, 2, DH, DH),
            buf(2, 3, 2, DH, DH), buf(2, 2, DH, DH), buf(2, DH, DH),
            buf(2, T, DH), buf(2, T, DH), buf(2, T, DH),
            DMA((140,)), DMA((NC,)), DMA((NH, 2)), DMA((2,)), DMA((2,)), DMA((2, NH)),
            DMA((NH, 2)), DMA((8,)), DMA((4,)), DMA((3,)), DMA((2, 8)), DMA((2, 4)),
            DMA((2, 3)), DMA((3,)), DMA((2,)), DMA((4,)),
        ],
        compiler_params=params(0),
        name="step",
    )(stride_offset, queries, keys, values, grad_out, w_out)
    return pl.pallas_call(
        hand_over, out_shape=shapes, in_specs=[VM] * 5, out_specs=(VM,) * 5, name="hand_over",
    )(*results)


def solution(mesh):
    return jax.shard_map(
        body,
        mesh=mesh,
        in_specs=(P("ctx", "head"), P("ctx", "head"), P("ctx", "head"), P("head"),
                  P("head", None), P("ctx", "head")),
        out_specs=(P("ctx", "head"), P("ctx", "head"), P("ctx", "head"), P("ctx", "head"),
                   P("head", "ctx")),
        check_vma=False,
    )
```

```python
import jax
import jax.numpy as jnp
from jax import lax
from jax.experimental import pallas as pl
from jax.experimental.pallas import tpu as pltpu
from jax.sharding import PartitionSpec as P

T = 512
DH = 128
BLK = 64
NH = 8
NC = 32
SCALE = DH ** -0.5
EXP2_SCALE = SCALE * 1.4426950408889634
NEG = -1e30
MESH = pl.DeviceIdType.MESH
BF = jnp.bfloat16
F32 = jnp.float32


def where_am_i():
    c = lax.axis_index("ctx")
    h = lax.axis_index("head")
    return c, h, c // 4, (c // 2) % 2, c % 2


def ctx_id(z, yh, core):
    return z * 4 + yh * 2 + core


def across(h):
    return h + 1 - 2 * lax.rem(h, 2)


def head_peers(h):
    return lax.rem(h + 2, NH), lax.rem(h + NH - 2, NH), across(h)


def signal(barrier, c, h):
    pl.semaphore_signal(barrier, inc=1, device_id=(c, h), device_id_type=MESH)


class Sends:
    def __init__(self, sems):
        self.sems, self.made = sems, []

    def start(self, src, dst, recv, c, h):
        copy = pltpu.make_async_remote_copy(
            src_ref=src, dst_ref=dst, send_sem=self.sems.at[len(self.made)],
            recv_sem=recv, device_id=(c, h), device_id_type=MESH)
        copy.start()
        self.made.append(copy)

    def finish(self):
        for copy in self.made:
            copy.wait_send()


def arrived(ref, recv, send, c, h):
    pltpu.make_async_remote_copy(
        src_ref=ref, dst_ref=ref, send_sem=send, recv_sem=recv,
        device_id=(c, h), device_id_type=MESH).wait_recv()


def fold(x, op):
    return op(x.reshape(T // 8, 8, T), axis=0)


def nt(a, b):
    return lax.dot_general(a, b, (((1,), (1,)), ((), ())), preferred_element_type=F32)


def tn(a, b):
    return lax.dot_general(a, b, (((0,), (0,)), ((), ())), preferred_element_type=F32)


def nn(a, b):
    return jnp.dot(a, b, preferred_element_type=F32)


def step_kernel(off_ref, q_ref, k_ref, v_ref, g_ref, w_ref,
                lo_ref, gq_ref, gk_ref, gv_ref, gw_ref,
                picked, near, fg, att_all, wc, gpick, gnear,
                qs, scores, probs, dnear, top, inv, acc, dog, gatt, rdot,
                wts, pair_w, wup, wdown, wdone, wslot,
                pair_p, mine, up, down, done, yslot, brecv, csum, crecv,
                send, pk_recv, g_recv, c_recv, b_recv, w_recv, a_recv,
                pw_recv, wup_recv, wdown_recv, pp_recv, up_recv, down_recv,
                y_recv, near_recv, local):
    c, h, z, yh, core = where_am_i()
    partner = c + 1 - 2 * core
    ypeer = ctx_id(z, 1 - yh, core)
    after, before = lax.rem(c + 2, NC), lax.rem(c + NC - 2, NC)
    above = ctx_id(lax.rem(z + 1, 8), yh, core)
    below = ctx_id(lax.rem(z + 7, 8), yh, core)
    east, west, side = head_peers(h)
    west_side, east_side, far = across(west), across(east), head_peers(east)[0]
    far_side = across(far)
    hs = [lax.rem(h + d, NH) for d in range(1, NH)]
    barrier = pltpu.get_barrier_semaphore()

    def owner(d, y):
        return ctx_id(lax.rem(z + d, 8), lax.rem(yh + y, 2), core)

    for peer in (partner, ypeer, after, before, above, below):
        signal(barrier, peer, h)
    for peer in hs:
        signal(barrier, c, peer)
    for r in range(2):
        wanted = jnp.full((BLK, DH), 7 - off_ref[r], jnp.int32)
        for source, slot in ((k_ref, r), (v_ref, 2 + r)):
            rows = source[:BLK].astype(F32)
            for b in range(1, 8):
                rows = jnp.where(wanted == b, source[b * BLK:(b + 1) * BLK].astype(F32), rows)
            picked[slot, c] = rows.astype(BF)
    copies = [
        pltpu.make_async_copy(k_ref, near.at[0, 0], local.at[0]),
        pltpu.make_async_copy(v_ref, near.at[1, 0], local.at[1]),
        pltpu.make_async_copy(g_ref, fg.at[h], local.at[2]),
        pltpu.make_async_copy(
            w_ref.at[:, pl.ds(pl.multiple_of(h * T, T), T)],
            wc.at[pl.ds(pl.multiple_of(h * 256, 256), 256), :], local.at[3]),
    ]
    for copy in copies:
        copy.start()
    for r in range(2):
        qs[r] = q_ref[:, r * DH:(r + 1) * DH]
    dnear[...] = jnp.zeros_like(dnear)
    def tile(p):
        return pl.ds(pl.multiple_of(p * 8, 8), 8)

    def own_scores(r):
        key = lax.broadcasted_iota(jnp.int32, (T, T), 0)
        query = lax.broadcasted_iota(jnp.int32, (T, T), 1)
        s = jnp.where(key <= query, nt(k_ref[...], qs[r]), NEG)
        scores[r, 0] = s
        top[r] = fold(s, jnp.max)

    def last_scores(r):
        s = jnp.where(c >= 1, nt(near[0, 1], qs[r]), NEG)
        scores[r, 1] = s
        top[r] = jnp.maximum(top[r], fold(s, jnp.max))

    def edge_scores(r):
        kb = lax.broadcasted_iota(jnp.int32, (T, T), 0) // BLK
        qb = lax.broadcasted_iota(jnp.int32, (T, T), 1) // BLK
        ok = ((kb > qb) | (kb == 7 - off_ref[r])) & (c >= 2)
        s = jnp.where(ok, nt(near[0, 2], qs[r]), NEG)
        scores[r, 2] = s
        top[r] = jnp.maximum(top[r], fold(s, jnp.max))

    def forward(r):
        def pick_scores(p, _):
            rows = lax.broadcasted_iota(jnp.int32, (T, T), 0)
            s = nt(picked[r, tile(p)].reshape(T, DH), qs[r])
            s = jnp.where(rows < (c - 2) * BLK - p * T, s, NEG)
            scores[r, 3 + p] = s
            top[r] = jnp.maximum(top[r], fold(s, jnp.max))
            return 0

        lax.fori_loop(0, 4, pick_scores, 0)
        m = jnp.max(top[r], axis=0, keepdims=True)
        top[r] = jnp.zeros((8, T), F32)
        acc[r] = jnp.zeros((DH, T), F32)

        def weigh(i, values):
            w = jnp.exp2((scores[r, i] - m) * EXP2_SCALE)
            top[r] += fold(w, jnp.sum)
            w = w.astype(BF)
            probs[r, i] = w
            acc[r] += tn(values, w)

        def near_mix(i, _):
            weigh(i, near[1, i])
            return 0

        def pick_mix(p, _):
            weigh(3 + p, picked[2 + r, tile(p)].reshape(T, DH))
            return 0

        lax.fori_loop(0, 3, near_mix, 0)
        lax.fori_loop(0, 4, pick_mix, 0)
        total = 1.0 / jnp.sum(top[r], axis=0, keepdims=True)
        inv[r] = jnp.broadcast_to(total, (8, T))
        att_all[h, pl.ds(r * DH, DH), :] = (acc[r] * total).astype(BF)

    def grad_att(r, block):
        gatt[...] += nt(w_ref[:, pl.ds(pl.multiple_of(r * T, T), T)], block)

    own_scores(0)
    own_scores(1)
    gatt[...] = jnp.zeros_like(gatt)
    grad_att(h, g_ref[...])
    pl.semaphore_wait(barrier, 13)

    sends = Sends(send)

    def block(t):
        return picked.at[:, t]

    def pass_on(t, *peers):
        for peer in peers:
            sends.start(block(t), block(t), pk_recv.at[t], peer, h)

    def take(t, peer):
        arrived(block(t), pk_recv.at[t], send.at[0], peer, h)

    def gpart(n, half):
        return fg.at[n, pl.ds(half * 256, 256)]

    def own_part(half, peer):
        sends.start(g_ref.at[pl.ds(half * 256, 256)], gpart(h, half), g_recv.at[h, half], c, peer)

    def grelay(n, half, source, *peers):
        arrived(gpart(n, half), g_recv.at[n, half], send.at[0], c, source)
        for peer in peers:
            sends.start(gpart(n, half), gpart(n, half), g_recv.at[n, half], c, peer)

    def pick_ring(step):
        for y in range(2):
            t = owner(8 - step, y)
            take(t, below)
            pass_on(t, *((above, partner) if step < 4 else (partner,)))
            if step < 4:
                t = owner(step, y)
                take(t, above)
                pass_on(t, *((below, partner) if step < 3 else (partner,)))

    pass_on(c, ypeer, above, below, partner)
    own_part(0, east)
    own_part(1, west)
    own_part(0, side)
    sends.start(k_ref, near.at[0, 2], c_recv.at[0], after, h)
    sends.start(v_ref, near.at[1, 2], c_recv.at[1], after, h)
    own_part(1, east)
    own_part(0, west)
    own_part(1, side)
    take(ypeer, ypeer)
    pass_on(ypeer, above, below, partner)
    pick_ring(1)
    grelay(side, 0, side, east, west)
    grelay(west, 0, west, east)
    grelay(east, 1, east, west)
    pick_ring(2)
    for n in range(2):
        arrived(near.at[n, 2], c_recv.at[n], send.at[0], before, h)
    for copy in copies:
        copy.wait()
    for n in range(2):
        sends.start(near.at[n, 2 * core], near.at[n, 1], b_recv.at[n], partner, h)
    edge_scores(0)
    pick_ring(3)
    edge_scores(1)
    grelay(side, 1, side, west, east)
    grad_att(side, fg[side])
    pick_ring(4)
    grelay(west_side, 0, west, east)
    grelay(east_side, 1, east, west)
    flip = 1 - 2 * core
    for n in range(2):
        arrived(near.at[n, 1], b_recv.at[n], send.at[0], partner, h)
    last_scores(0)
    last_scores(1)
    for d in range(8):
        for y in range(2):
            t = owner(d, y) + flip
            take(t, partner)

    def part(n, half):
        return att_all.at[n, pl.ds(half * DH, DH)]

    def relay(n, half, source, *peers):
        if source is not None:
            arrived(part(n, half), a_recv.at[n, half], send.at[0], c, source)
        for peer in peers:
            sends.start(part(n, half), part(n, half), a_recv.at[n, half], c, peer)

    def piece(half, r):
        return wc.at[pl.ds(pl.multiple_of(r * 256, 256), 256),
                     pl.ds(pl.multiple_of(half * 256, 256), 256)]

    forward(0)
    relay(h, 0, None, east, side, west)
    forward(1)
    relay(h, 1, None, west, side, east)
    for n, half, source in (
            (west, 1, west), (east, 0, east), (west_side, 1, west), (east_side, 0, east),
            (far, 0, west), (far, 1, east), (far_side, 0, west), (far_side, 1, east)):
        grelay(n, half, source)
    for n in (west, east, west_side, east_side, far, far_side):
        grad_att(n, fg[n])

    order = [lax.rem(z + d, 8) for d in (4, 5, 3, 6, 2, 7, 1, 0)]
    for t in order:
        term = nn(att_all[h], fg[t])
        for j in range(4):
            wts[t, j % 2, j // 2] = term[:, j * DH:(j + 1) * DH].astype(BF)
        sends.start(wts.at[t, 1 - core], pair_w.at[t], pw_recv.at[t], partner, h)

    def quad(p):
        return pl.ds(pl.multiple_of(p * 4, 4), 4)

    def combine(t):
        arrived(pair_w.at[t], pw_recv.at[t], send.at[0], partner, h)
        wts[t, core] = (wts[t, core].astype(F32) + pair_w[t].astype(F32)).astype(BF)

    def grads(r, i, keys, values):
        w = probs[r, i]
        do = dog[r]
        dp = nt(values, do)
        ds = (w.astype(F32) * (dp - rdot[r, 0:1])).astype(BF)
        acc[r] += tn(keys, ds)
        return nn(ds, qs[r]) * SCALE, nn(w, do)

    def start_backward(r):
        rows = pl.ds(r * DH, DH)
        grad = gatt[rows, :].astype(BF).astype(F32)
        total = inv[r, 0:1]
        dog[r] = (grad * total).T.astype(BF)
        acc[r] = jnp.zeros((DH, T), F32)
        rdot[r] = jnp.broadcast_to(
            jnp.sum(grad * att_all[h, rows, :].astype(F32), axis=0, keepdims=True) * total, (8, T))

    def backward_near(r, first, last):
        def near_grads(i, _):
            dk, dv = grads(r, i, near[0, i], near[1, i])
            dnear[0, i] += dk
            dnear[1, i] += dv
            return 0

        lax.fori_loop(first, last, near_grads, 0)

    def backward_pick(r):
        def pick_grads(p, _):
            dk, dv = grads(r, 3 + p, picked[r, tile(p)].reshape(T, DH),
                           picked[2 + r, tile(p)].reshape(T, DH))
            gpick[r, 0, quad(p)] = dk.astype(BF).reshape(4, 2, BLK, DH)
            gpick[r, 1, quad(p)] = dv.astype(BF).reshape(4, 2, BLK, DH)
            return 0

        lax.fori_loop(0, 4, pick_grads, 0)

    def w_ring(step):
        t = order[2 + 2 * step]
        combine(t)
        arrived(wup.at[step], wup_recv.at[step], send.at[0], below, h)
        wup[step] = (wup[step].astype(F32) + wts[t, core].astype(F32)).astype(BF)
        sends.start(wup.at[step], wup.at[step + 1], wup_recv.at[step + 1], above, h)
        t = order[3 + 2 * step]
        combine(t)
        if step < 2:
            arrived(wdown.at[step], wdown_recv.at[step], send.at[0], above, h)
            wdown[step] = (wdown[step].astype(F32) + wts[t, core].astype(F32)).astype(BF)
            sends.start(wdown.at[step], wdown.at[step + 1], wdown_recv.at[step + 1], below, h)

    def pair(t):
        return pl.ds(pl.multiple_of(t * 2, 2), 2)

    def share_picks(r):
        for t in order:
            sends.start(gpick.at[r, :, pair(t), 1 - core], pair_p.at[r, t], pp_recv.at[r, t],
                        partner, h)

    def combine_picks(r, t):
        arrived(pair_p.at[r, t], pp_recv.at[r, t], send.at[0], partner, h)
        for y in range(2):
            own = gpick[r, :, t * 2 + y, core].astype(F32) + pair_p[r, t, :, y].astype(F32)
            mine[r, t, y] = own.astype(BF).reshape(DH, DH)

    def open_ring(r):
        combine_picks(r, order[0])
        sends.start(mine.at[r, order[0]], up.at[r, 0], up_recv.at[r, 0], above, h)
        combine_picks(r, order[1])
        sends.start(mine.at[r, order[1]], down.at[r, 0], down_recv.at[r, 0], below, h)

    def sum_ring(r, step):
        t = order[2 + 2 * step]
        combine_picks(r, t)
        arrived(up.at[r, step], up_recv.at[r, step], send.at[0], below, h)
        up[r, step] = (up[r, step].astype(F32) + mine[r, t].astype(F32)).astype(BF)
        sends.start(up.at[r, step], up.at[r, step + 1], up_recv.at[r, step + 1], above, h)
        t = order[3 + 2 * step]
        combine_picks(r, t)
        if step < 2:
            arrived(down.at[r, step], down_recv.at[r, step], send.at[0], above, h)
            down[r, step] = (down[r, step].astype(F32) + mine[r, t].astype(F32)).astype(BF)
            sends.start(down.at[r, step], down.at[r, step + 1], down_recv.at[r, step + 1],
                        below, h)

    def close_ring(r):
        arrived(down.at[r, 2], down_recv.at[r, 2], send.at[0], above, h)
        arrived(up.at[r, 3], up_recv.at[r, 3], send.at[0], below, h)
        done[r] = (mine[r, z].astype(F32) + up[r, 3].astype(F32)
                   + down[r, 2].astype(F32)).astype(BF)
        sends.start(done.at[r, 1 - yh], yslot.at[r], y_recv.at[r], ypeer, h)

    start_backward(0)
    relay(side, 0, side, east, west)
    relay(west, 0, west, east)
    combine(order[0])
    sends.start(wts.at[order[0], core], wup.at[0], wup_recv.at[0], above, h)
    combine(order[1])
    sends.start(wts.at[order[1], core], wdown.at[0], wdown_recv.at[0], below, h)
    backward_pick(0)
    share_picks(0)
    relay(side, 1, side, west, east)
    relay(east, 1, east, west)
    w_ring(0)
    for peer in hs:
        sends.start(w_ref.at[:, pl.ds(pl.multiple_of(peer * T + core * 256, 256), 256)],
                    piece(core, h), w_recv.at[core, h], c, peer)
    backward_near(0, 1, 3)
    relay(west_side, 0, west, east)
    relay(east_side, 1, east, west)
    w_ring(1)
    open_ring(0)
    start_backward(1)
    backward_pick(1)
    share_picks(1)
    w_ring(2)
    sum_ring(0, 0)
    backward_near(1, 1, 3)
    gnear[:, 1:] = dnear[:, 1:].astype(BF)
    sends.start(gnear.at[:, 1], brecv, near_recv.at[0], partner, h)
    open_ring(1)
    sum_ring(0, 1)
    backward_near(0, 0, 1)
    arrived(brecv, near_recv.at[0], send.at[0], partner, h)
    extra = brecv[...].astype(F32)
    csum[...] = (gnear[:, 2].astype(F32) + jnp.where(core == 1, extra, 0.0)).astype(BF)
    sends.start(csum, crecv, near_recv.at[1], before, h)
    sum_ring(1, 0)
    backward_near(1, 0, 1)
    arrived(wdown.at[2], wdown_recv.at[2], send.at[0], above, h)
    arrived(wup.at[3], wup_recv.at[3], send.at[0], below, h)
    wdone[...] = (wts[z, core].astype(F32) + wup[3].astype(F32)
                  + wdown[2].astype(F32)).astype(BF)
    sends.start(wdone.at[1 - yh], wslot, y_recv.at[2], ypeer, h)
    for r in range(2):
        gq_ref[:, r * DH:(r + 1) * DH] = (acc[r].T * SCALE).astype(BF)
    sum_ring(0, 2)
    sum_ring(1, 1)
    close_ring(0)
    relay(west, 1, west)
    relay(east, 0, east)
    relay(west_side, 1, west)
    relay(east_side, 0, east)
    relay(far, 0, west)
    relay(far, 1, east)
    relay(far_side, 0, west)
    relay(far_side, 1, east)
    for peer in hs:
        arrived(piece(core, peer), w_recv.at[core, peer], send.at[0], c, peer)
        sends.start(piece(core, peer), piece(core, peer), w_recv.at[core, peer], partner, h)
    sum_ring(1, 2)
    close_ring(1)
    for peer in hs:
        arrived(piece(1 - core, peer), w_recv.at[1 - core, peer], send.at[0], partner, h)
    scores[0, 0] = jnp.zeros((T, T), F32)

    def project(r, _):
        scores[0, 0] += tn(att_all[r], wc[pl.ds(pl.multiple_of(r * 256, 256), 256), :])
        return 0

    lax.fori_loop(0, NH, project, 0)
    lo_ref[...] = scores[0, 0].astype(BF)
    arrived(wslot, y_recv.at[2], send.at[0], ypeer, h)
    gw_ref[...] = (wdone[yh].astype(F32) + wslot[...].astype(F32)).astype(BF)
    arrived(crecv, near_recv.at[1], send.at[0], after, h)
    grad = dnear[:, 0] + jnp.where(core == 1, 0.0, extra) + crecv[...].astype(F32)
    block = lax.broadcasted_iota(jnp.int32, (T, DH), 0) // BLK
    grads_out = [grad[0], grad[1]]
    for r in range(2):
        arrived(yslot.at[r], y_recv.at[r], send.at[0], ypeer, h)
        total = done[r, yh].astype(F32) + yslot[r].astype(F32)
        for n in range(2):
            spread = jnp.concatenate([total[n * BLK:(n + 1) * BLK]] * 8, axis=0)
            grads_out[n] += jnp.where(block == 7 - off_ref[r], spread, 0.0)
    gk_ref[...] = grads_out[0].astype(BF)
    gv_ref[...] = grads_out[1].astype(BF)
    sends.finish()


def hand_over(*refs):
    for source, target in zip(refs[:5], refs[5:]):
        target[...] = source[...]


VM = pl.BlockSpec(memory_space=pltpu.VMEM)
SM = pl.BlockSpec(memory_space=pltpu.SMEM)
DMA = pltpu.SemaphoreType.DMA


def shaped(*shape, dtype=BF):
    return jax.ShapeDtypeStruct(shape, dtype)


def params(number):
    return pltpu.CompilerParams(
        collective_id=number, has_side_effects=True, vmem_limit_bytes=60 << 20)


def buf(*shape, dtype=BF):
    return pltpu.VMEM(shape, dtype)


def body(queries, keys, values, stride_offset, w_out, grad_out):
    shapes = (shaped(T, T), shaped(T, 256), shaped(T, DH), shaped(T, DH), shaped(256, DH))
    results = pl.pallas_call(
        step_kernel,
        out_shape=shapes,
        in_specs=[SM, VM, VM, VM, VM, VM],
        out_specs=(VM,) * 5,
        scratch_shapes=[
            buf(4, NC, BLK, DH), buf(2, 3, T, DH), buf(NH, T, T), buf(NH, 256, T),
            buf(2048, T), buf(2, 2, 16, 2, BLK, DH), buf(2, 3, T, DH),
            buf(2, T, DH), buf(2, 7, T, T, dtype=F32), buf(2, 7, T, T),
            buf(2, 3, T, DH, dtype=F32), buf(2, 8, T, dtype=F32), buf(2, 8, T, dtype=F32),
            buf(2, DH, T, dtype=F32), buf(2, T, DH), buf(256, T, dtype=F32), buf(2, 8, T, dtype=F32),
            buf(8, 2, 2, 256, DH), buf(8, 2, 256, DH), buf(4, 2, 256, DH), buf(3, 2, 256, DH),
            buf(2, 256, DH), buf(256, DH),
            buf(2, 8, 2, 2, BLK, DH), buf(2, 8, 2, DH, DH), buf(2, 4, 2, DH, DH),
            buf(2, 3, 2, DH, DH), buf(2, 2, DH, DH), buf(2, DH, DH),
            buf(2, T, DH), buf(2, T, DH), buf(2, T, DH),
            DMA((140,)), DMA((NC,)), DMA((NH, 2)), DMA((2,)), DMA((2,)), DMA((2, NH)),
            DMA((NH, 2)), DMA((8,)), DMA((4,)), DMA((3,)), DMA((2, 8)), DMA((2, 4)),
            DMA((2, 3)), DMA((3,)), DMA((2,)), DMA((4,)),
        ],
        compiler_params=params(0),
        name="step",
    )(stride_offset, queries, keys, values, grad_out, w_out)
    return pl.pallas_call(
        hand_over, out_shape=shapes, in_specs=[VM] * 5, out_specs=(VM,) * 5, name="hand_over",
    )(*results)


def solution(mesh):
    return jax.shard_map(
        body,
        mesh=mesh,
        in_specs=(P("ctx", "head"), P("ctx", "head"), P("ctx", "head"), P("head"),
                  P("head", None), P("ctx", "head")),
        out_specs=(P("ctx", "head"), P("ctx", "head"), P("ctx", "head"), P("ctx", "head"),
                   P("head", "ctx")),
        check_vma=False,
    )
```
